32 devices in a mesh: seq: 8 (over z, x), tp: 4 (over y, core).
Axes of the slice: x: 2, y: 2, z: 4, core: 2. Of those that a mesh axis runs over, the one named last changes fastest.
Arguments:
- block_in: bfloat16 [2, 1024, 1024], P(None, 'seq', 'tp'), may hold values from -6 to 6
- out_grad: bfloat16 [2, 1024, 1024], P(None, 'seq', 'tp'), may hold values from -6 to 6
- decay_code: int32 [2, 1024, 8], P(None, 'seq', 'tp'), may hold values from 0 to 14
- beta_code: int32 [2, 1024, 8], P(None, 'seq', 'tp'), may hold values from 0 to 7
- norm_gain: bfloat16 [1024], P('seq'), may hold values from 0.5 to 1.5
- w_query: bfloat16 [1024, 1024], P('seq', 'tp'), may hold values from -0.1875 to 0.1875
- w_key: bfloat16 [1024, 1024], P('seq', 'tp'), may hold values from -0.1875 to 0.1875
- w_value: bfloat16 [1024, 2048], P('seq', 'tp'), may hold values from -0.1875 to 0.1875
- w_outgate: bfloat16 [1024, 2048], P('seq', 'tp'), may hold values from -0.1875 to 0.1875
- conv_query: bfloat16 [4, 8, 128], P(None, 'tp', 'seq'), may hold values from -3 to 3
- conv_key: bfloat16 [4, 8, 128], P(None, 'tp', 'seq'), may hold values from -3 to 3
- conv_value: bfloat16 [4, 8, 256], P(None, 'tp', 'seq'), may hold values from -3 to 3
- head_gain: bfloat16 [8, 256], P('tp', 'seq'), may hold values from 0.5 to 1.5
- w_output: bfloat16 [2048, 1024], P('tp', 'seq'), may hold values from -0.125 to 0.125
- mlp_gain: bfloat16 [1024], P('seq'), may hold values from 0.5 to 1.5
- w_gate: bfloat16 [1024, 2816], P('seq', 'tp'), may hold values from -0.1875 to 0.1875
- w_up: bfloat16 [1024, 2816], P('seq', 'tp'), may hold values from -0.1875 to 0.1875
- w_down: bfloat16 [2816, 1024], P('tp', 'seq'), may hold values from -0.109375 to 0.109375
Outputs:
- block_out: bfloat16 [2, 1024, 1024], P(None, 'seq', 'tp')
- grad_in: float32 [2, 1024, 1024], P(None, 'seq', 'tp')
- grad_norm_gain: float32 [1024], P('seq')
- grad_query: float32 [1024, 1024], P('seq', 'tp')
- grad_key: float32 [1024, 1024], P('seq', 'tp')
- grad_value: float32 [1024, 2048], P('seq', 'tp')
- grad_outgate: float32 [1024, 2048], P('seq', 'tp')
- grad_conv_query: float32 [4, 8, 128], P(None, 'tp', 'seq')
- grad_conv_key: float32 [4, 8, 128], P(None, 'tp', 'seq')
- grad_conv_value: float32 [4, 8, 256], P(None, 'tp', 'seq')
- grad_head_gain: float32 [8, 256], P('tp', 'seq')
- grad_output: float32 [2048, 1024], P('tp', 'seq')
- grad_mlp_gain: float32 [1024], P('seq')
- grad_gate: float32 [1024, 2816], P('seq', 'tp')
- grad_up: float32 [1024, 2816], P('seq', 'tp')
- grad_down: float32 [2816, 1024], P('tp', 'seq')
The draws below stay inside these ranges and needn't reach their ends.
All inputs are finite; a program needn't handle non-finite values.
Results may differ from the reference program's by a relative error of at most 0.019.
Values may be sent and summed in bfloat16 or wider, within the bound.
A program may use at most 128 MiB of HBM per device.

```python
import jax
import jax.numpy as jnp
from jax import lax

D = 1024
H = 8
DK = 128
DV = 256
FF = 2816
CONV = 4
BLOCK = 64
SEQS = 2
SEQUENCE_LENGTH = 1024
HK = 1024
HV = 2048


def draw_decay_code(key, part):
    ranking = jax.random.permutation(jax.random.fold_in(key, 12), H)
    base_level = 4 + ranking * 9 // (H - 1)
    offsets = jax.random.randint(jax.random.fold_in(key, 13), (SEQS, SEQUENCE_LENGTH, H), 0, 2)
    offsets = offsets.at[:, 0, :].set(1)
    quantized_levels = base_level[None, None, :] + offsets
    locations = jax.random.randint(jax.random.fold_in(key, 14), (SEQS, 6), 1, SEQUENCE_LENGTH)
    event_mask = jnp.any(jnp.arange(SEQUENCE_LENGTH)[None, :, None] == locations[:, None, :], axis=2)
    return jnp.where(event_mask[:, :, None], 0, quantized_levels).astype(jnp.int32)


def set_ends(entries, key, least, largest):
    index_at = [jax.random.randint(jax.random.fold_in(key, axis), (), 0, length) for axis, length in enumerate(entries.shape)]
    longest = entries.shape.index(max(entries.shape))
    next_to = index_at[:longest] + [(index_at[longest] + 1) % entries.shape[longest]] + index_at[longest + 1:]
    return entries.at[tuple(index_at)].set(least).at[tuple(next_to)].set(largest)


def strengthened(drawn, own_key, source, target, parts, factor):
    owner, partner = [(jnp.arange(drawn.shape[position]) // (drawn.shape[position] // parts)).reshape([-1 if axis == position else 1 for axis in range(drawn.ndim)]) for position in (source, target)]
    chosen = jax.random.permutation(own_key, parts)[partner]
    strong = (owner == chosen) | (owner == (partner + parts // 2) % parts)
    return jnp.where(strong, factor * drawn, drawn)


def shard_levels(rng, extent, cuts, low, top_value):
    def one(position, shards_of):
        draws = jax.random.uniform(jax.random.fold_in(jax.random.fold_in(rng, 6), position), (shards_of,), jnp.float32, low / len(cuts), top_value / len(cuts))
        return jnp.repeat(jnp.exp(draws), extent[position] // shards_of).reshape((-1,) + (1,) * (len(extent) - position - 1))

    factor_of = one(*cuts[0])
    for cut in cuts[1:]:
        factor_of = factor_of * one(*cut)
    return factor_of


def noise(stream_key, dims, scale, most, cuts=(), kind=jnp.bfloat16):
    factor_of = shard_levels(stream_key, dims, cuts, -0.22, 0.18) if cuts else 1.0
    values = jax.random.normal(stream_key, dims, jnp.float32) * scale * factor_of
    return jnp.minimum(jnp.maximum(values, -most), most).astype(kind)


def gaussian_with(stream_key, extent, deviation, limit, cuts, heavy, held_as=jnp.bfloat16):
    array = deviation * jax.random.normal(stream_key, extent, jnp.float32)
    if cuts:
        array = array * shard_levels(stream_key, extent, cuts, -0.22, 0.18)
    return jnp.clip(strengthened(array, jax.random.fold_in(stream_key, 3), *heavy), -limit, limit).astype(held_as)


def setup_inputs(seed: int = 0) -> dict:
    streams_of = jax.random.split(jax.random.key(seed), 19)
    block_in = gaussian_with(streams_of[0], (SEQS, SEQUENCE_LENGTH, D), 1.0, 6.0, ((1, 8), (2, 4)), (1, 2, 8, 2.0))
    out_grad = gaussian_with(streams_of[1], (SEQS, SEQUENCE_LENGTH, D), 1.0, 6.0, ((1, 8), (2, 4)), (1, 2, 8, 2.0))
    decay_code = draw_decay_code(jax.random.fold_in(streams_of[18], 71), 0)
    beta_code = set_ends(jax.random.randint(streams_of[3], (SEQS, SEQUENCE_LENGTH, H), 0, 8), jax.random.fold_in(streams_of[3], 1), 0, 7).astype(jnp.int32)
    norm_gain = jnp.clip(1.0 + 0.1 * jax.random.normal(streams_of[4], (D,), jnp.float32), 0.5, 1.5).astype(jnp.bfloat16)
    w_query = noise(streams_of[5], (D, HK), D ** -0.5, 0.1875, ((0, 8), (1, 4)))
    w_key = noise(streams_of[6], (D, HK), D ** -0.5, 0.1875, ((0, 8), (1, 4)))
    w_value = noise(streams_of[7], (D, HV), D ** -0.5, 0.1875, ((0, 8), (1, 4)))
    w_outgate = noise(streams_of[8], (D, HV), D ** -0.5, 0.1875, ((0, 8), (1, 4)))
    conv_query = noise(streams_of[9], (CONV, H, DK), CONV ** -0.5, 3.0, ((1, 4), (2, 8)))
    conv_key = noise(streams_of[10], (CONV, H, DK), CONV ** -0.5, 3.0, ((1, 4), (2, 8)))
    conv_value = noise(streams_of[11], (CONV, H, DV), CONV ** -0.5, 3.0, ((1, 4), (2, 8)))
    head_gain = jnp.clip(1.0 + 0.1 * jax.random.normal(streams_of[12], (H, DV), jnp.float32), 0.5, 1.5).astype(jnp.bfloat16)
    w_output = noise(streams_of[13], (HV, D), HV ** -0.5, 0.125, ((0, 4), (1, 8)))
    mlp_gain = jnp.clip(1.0 + 0.1 * jax.random.normal(streams_of[14], (D,), jnp.float32), 0.5, 1.5).astype(jnp.bfloat16)
    w_gate = noise(streams_of[15], (D, FF), D ** -0.5, 0.1875, ((0, 8), (1, 4)))
    w_up = noise(streams_of[16], (D, FF), D ** -0.5, 0.1875, ((0, 8), (1, 4)))
    w_down = noise(streams_of[17], (FF, D), FF ** -0.5, 0.109375, ((0, 4), (1, 8)))
    return {"block_in": block_in, "out_grad": out_grad, "decay_code": decay_code, "beta_code": beta_code, "norm_gain": norm_gain, "w_query": w_query, "w_key": w_key, "w_value": w_value, "w_outgate": w_outgate, "conv_query": conv_query, "conv_key": conv_key, "conv_value": conv_value, "head_gain": head_gain, "w_output": w_output, "mlp_gain": mlp_gain, "w_gate": w_gate, "w_up": w_up, "w_down": w_down}


PRECISE = lax.Precision.HIGHEST
EPSILON = 1e-06
LOG_TWO = 0.6931471805599453

def row_scale(values):
    return lax.rsqrt(lax.optimization_barrier(jnp.mean(values * values, axis=-1, keepdims=True)) + EPSILON)

def silu_slope(values):
    sigmoid = jax.nn.sigmoid(values)
    return sigmoid * (1.0 + values * (1.0 - sigmoid))

def norm_back(d_normed, inputs, scales, gains):
    weighted = d_normed * gains
    return scales * (weighted - inputs * scales * scales * lax.optimization_barrier(jnp.mean(weighted * inputs, axis=-1, keepdims=True)))

def unit_inverse(strict_part):
    width = strict_part.shape[-1]
    negated = -strict_part
    result = jnp.eye(width, dtype=strict_part.dtype) + negated
    for rounds in range(width.bit_length() - 2):
        negated = jnp.matmul(negated, negated, precision=PRECISE)
        result = result + jnp.matmul(result, negated, precision=PRECISE)
    return result

def group_step(state_in, query, keys, values, log_decay, write_strength_rate):
    width = log_decay.shape[-1]
    cumulative = jnp.cumsum(log_decay, axis=-1)
    locations = jnp.arange(width)
    strictly = (locations[:, None] > locations[None, :]).astype(state_in.dtype)
    up_to = locations[:, None] >= locations[None, :]
    spread = cumulative[..., :, None] - cumulative[..., None, :]
    factors = jnp.exp(jnp.where(up_to, spread, 0.0)) * up_to.astype(state_in.dtype)
    key_dots = jnp.einsum('...td,...sd->...ts', keys, keys, precision=PRECISE)
    inverse = unit_inverse(write_strength_rate[..., :, None] * key_dots * factors * strictly)
    growth = jnp.exp(cumulative)
    targets = write_strength_rate[..., None] * (values - growth[..., None] * jnp.einsum('...td,...dw->...tw', keys, state_in, precision=PRECISE))
    update = jnp.matmul(inverse, targets, precision=PRECISE)
    scores = jnp.einsum('...td,...sd->...ts', query, keys, precision=PRECISE) * factors
    output = growth[..., None] * jnp.einsum('...td,...dw->...tw', query, state_in, precision=PRECISE) + jnp.matmul(scores, update, precision=PRECISE)
    final_log = cumulative[..., -1:]
    carried = jnp.exp(final_log)[..., None] * state_in + jnp.einsum('...sd,...sw->...dw', keys * jnp.exp(final_log - cumulative)[..., None], update, precision=PRECISE)
    return (carried, output)

def delta_run(state_in, query, keys, values, log_decay, write_strength_rate):
    leading = query.shape[:-2]
    length = query.shape[-2]
    blocks = length // BLOCK
    axis_at = len(leading)

    def split_blocks(tensor):
        tensor = tensor.reshape(leading + (blocks, BLOCK) + tensor.shape[axis_at + 1:])
        return jnp.moveaxis(tensor, axis_at, 0)

    def advance(carried, pieces):
        return jax.checkpoint(group_step)(carried, *pieces)
    end_state, outputs = lax.scan(advance, state_in, (split_blocks(query), split_blocks(keys), split_blocks(values), split_blocks(log_decay), split_blocks(write_strength_rate)))
    outputs = jnp.moveaxis(outputs, 0, axis_at)
    return (outputs.reshape(leading + (length, outputs.shape[-1])), end_state)

def conv_valid(kernel, extended):
    length = extended.shape[1] - kernel.shape[0] + 1
    return sum((kernel[offset] * extended[:, offset:offset + length] for offset in range(kernel.shape[0])))

def heads_first(tensor, width):
    shaped = tensor.reshape(tensor.shape[0], tensor.shape[1], -1, width)
    return jnp.transpose(shaped, (0, 2, 1, 3))

def rows_last(tensor):
    shaped = jnp.transpose(tensor, (0, 2, 1, 3))
    return shaped.reshape(shaped.shape[0], shaped.shape[1], -1)

def activate(kern_query, kern_key, kern_value, ext_query, ext_key, ext_value):
    query = heads_first(jax.nn.silu(conv_valid(kern_query, ext_query)), DK)
    query = query * lax.rsqrt(lax.optimization_barrier(jnp.sum(query * query, axis=-1, keepdims=True)) + EPSILON) * DK ** (-0.5)
    keys = heads_first(jax.nn.silu(conv_valid(kern_key, ext_key)), DK)
    keys = keys * lax.rsqrt(lax.optimization_barrier(jnp.sum(keys * keys, axis=-1, keepdims=True)) + EPSILON)
    values = heads_first(jax.nn.silu(conv_valid(kern_value, ext_value)), DV)
    return (query, keys, values)

def gate_rates(decay_code, beta_code):
    log_decay = -0.5 * jnp.exp(-LOG_TWO * decay_code.astype(jnp.float32))
    write_strength_rate = (beta_code.astype(jnp.float32) + 1.0) / 8.0
    return (jnp.moveaxis(log_decay, 2, 1), jnp.moveaxis(write_strength_rate, 2, 1))

def reference(block_in, out_grad, decay_code, beta_code, norm_gain, w_query, w_key, w_value, w_outgate, conv_query, conv_key, conv_value, head_gain, w_output, mlp_gain, w_gate, w_up, w_down):
    residual = block_in.astype(jnp.float32).reshape(-1, D)
    scale_one = row_scale(residual)
    gain_one = norm_gain.astype(jnp.float32)
    normed = (residual * scale_one * gain_one).astype(jnp.bfloat16)
    proj_query = jnp.dot(normed, w_query, preferred_element_type=jnp.float32)
    proj_key = jnp.dot(normed, w_key, preferred_element_type=jnp.float32)
    proj_value = jnp.dot(normed, w_value, preferred_element_type=jnp.float32)
    proj_outgate = jnp.dot(normed, w_outgate, preferred_element_type=jnp.float32)

    def extend(tensor):
        return jnp.pad(tensor.reshape(SEQS, SEQUENCE_LENGTH, -1), ((0, 0), (CONV - 1, 0), (0, 0)))
    kernels = tuple((kernel.astype(jnp.float32).reshape(CONV, -1) for kernel in (conv_query, conv_key, conv_value)))
    extended = (extend(proj_query), extend(proj_key), extend(proj_value))
    log_decay, write_strength_rate = gate_rates(decay_code, beta_code)
    start_zero = jnp.zeros((SEQS, H, DK, DV), jnp.float32)

    def mixer(kern_query, kern_key, kern_value, ext_query, ext_key, ext_value):
        query, keys, values = activate(kern_query, kern_key, kern_value, ext_query, ext_key, ext_value)
        return delta_run(start_zero, query, keys, values, log_decay, write_strength_rate)[0]
    mixed, mixer_back = jax.vjp(mixer, kernels[0], kernels[1], kernels[2], extended[0], extended[1], extended[2])
    head_scale = row_scale(mixed)
    gain_head = head_gain.astype(jnp.float32)[None, :, None, :]
    head_out = mixed * head_scale * gain_head
    gate_pre = heads_first(proj_outgate.reshape(SEQS, SEQUENCE_LENGTH, -1), DV)
    gated = rows_last(head_out * jax.nn.silu(gate_pre)).reshape(-1, HV).astype(jnp.bfloat16)
    middle = residual + jnp.dot(gated, w_output, preferred_element_type=jnp.float32)
    scale_two = row_scale(middle)
    gain_two = mlp_gain.astype(jnp.float32)
    normed_two = (middle * scale_two * gain_two).astype(jnp.bfloat16)
    pre_gate = jnp.dot(normed_two, w_gate, preferred_element_type=jnp.float32)
    pre_up = jnp.dot(normed_two, w_up, preferred_element_type=jnp.float32)
    hidden = (jax.nn.silu(pre_gate) * pre_up).astype(jnp.bfloat16)
    block_out = (middle + jnp.dot(hidden, w_down, preferred_element_type=jnp.float32)).astype(jnp.bfloat16)
    cotangent = out_grad.reshape(-1, D)
    d_hidden = jnp.dot(cotangent, w_down.T, preferred_element_type=jnp.float32)
    grad_down = jnp.dot(hidden.T, cotangent, preferred_element_type=jnp.float32)
    d_pre_gate = (d_hidden * pre_up * silu_slope(pre_gate)).astype(jnp.bfloat16)
    d_pre_up = (d_hidden * jax.nn.silu(pre_gate)).astype(jnp.bfloat16)
    d_normed_two = jnp.dot(d_pre_gate, w_gate.T, preferred_element_type=jnp.float32) + jnp.dot(d_pre_up, w_up.T, preferred_element_type=jnp.float32)
    grad_gate = jnp.dot(normed_two.T, d_pre_gate, preferred_element_type=jnp.float32)
    grad_up = jnp.dot(normed_two.T, d_pre_up, preferred_element_type=jnp.float32)
    grad_mlp_gain = lax.optimization_barrier(jnp.sum(d_normed_two * middle * scale_two, axis=0))
    d_middle = cotangent.astype(jnp.float32) + norm_back(d_normed_two, middle, scale_two, gain_two)
    d_mid_low = d_middle.astype(jnp.bfloat16)
    d_gated = jnp.dot(d_mid_low, w_output.T, preferred_element_type=jnp.float32)
    grad_output = jnp.dot(gated.T, d_mid_low, preferred_element_type=jnp.float32)
    d_gated_heads = heads_first(d_gated.reshape(SEQS, SEQUENCE_LENGTH, -1), DV)
    d_outgate = rows_last(d_gated_heads * head_out * silu_slope(gate_pre)).reshape(-1, HV).astype(jnp.bfloat16)
    d_head = d_gated_heads * jax.nn.silu(gate_pre)
    grad_head_gain = lax.optimization_barrier(jnp.sum(d_head * mixed * head_scale, axis=(0, 2)))
    d_mixed = norm_back(d_head, mixed, head_scale, gain_head)
    mixer_grads = mixer_back(d_mixed)
    d_proj_query = mixer_grads[3][:, CONV - 1:].reshape(-1, HK).astype(jnp.bfloat16)
    d_proj_key = mixer_grads[4][:, CONV - 1:].reshape(-1, HK).astype(jnp.bfloat16)
    d_proj_value = mixer_grads[5][:, CONV - 1:].reshape(-1, HV).astype(jnp.bfloat16)
    d_normed = jnp.dot(d_proj_query, w_query.T, preferred_element_type=jnp.float32)
    d_normed = d_normed + jnp.dot(d_proj_key, w_key.T, preferred_element_type=jnp.float32)
    d_normed = d_normed + jnp.dot(d_proj_value, w_value.T, preferred_element_type=jnp.float32)
    d_normed = d_normed + jnp.dot(d_outgate, w_outgate.T, preferred_element_type=jnp.float32)
    grad_query = jnp.dot(normed.T, d_proj_query, preferred_element_type=jnp.float32)
    grad_key = jnp.dot(normed.T, d_proj_key, preferred_element_type=jnp.float32)
    grad_value = jnp.dot(normed.T, d_proj_value, preferred_element_type=jnp.float32)
    grad_outgate = jnp.dot(normed.T, d_outgate, preferred_element_type=jnp.float32)
    grad_norm_gain = lax.optimization_barrier(jnp.sum(d_normed * residual * scale_one, axis=0))
    grad_in = d_middle + norm_back(d_normed, residual, scale_one, gain_one)
    return (block_out.reshape(SEQS, SEQUENCE_LENGTH, D), grad_in.reshape(SEQS, SEQUENCE_LENGTH, D), grad_norm_gain, grad_query, grad_key, grad_value, grad_outgate, mixer_grads[0].reshape(CONV, H, DK), mixer_grads[1].reshape(CONV, H, DK), mixer_grads[2].reshape(CONV, H, DV), grad_head_gain, grad_output, grad_mlp_gain, grad_gate, grad_up, grad_down)
```

```python
import functools

import jax
import jax.numpy as jnp
from jax import lax
from jax.experimental import pallas as pl
from jax.experimental.pallas import tpu as pltpu
from jax.sharding import PartitionSpec as P

DK = 128
DV = 256
CONV = 4
HALO = 8
SMALL_ROWS = 16
EPSILON = 1e-06
LOG_TWO = 0.6931471805599453
MESH = pl.DeviceIdType.MESH
NN = ((1,), (0,))
NT = ((1,), (1,))
TN = ((0,), (0,))
BF = jnp.bfloat16
F32 = jnp.float32


def mm(a, b, dims=NN):
    return lax.dot_general(a, b, (dims, ((), ())), preferred_element_type=F32)


def halves(a):
    high = a.astype(BF)
    return high, (a - high.astype(F32)).astype(BF)


def mm3(a, b, dims=NN):
    a_high, a_low = halves(a)
    b_high, b_low = halves(b)
    return mm(a_high, b_high, dims) + (mm(a_high, b_low, dims) + mm(a_low, b_high, dims))


def mm2(a, b, dims=NN):
    a_high, a_low = halves(a)
    return mm(a_high, b, dims) + mm(a_low, b, dims)


def sigmoid(values):
    return 1.0 / (1.0 + jnp.exp(-values))


def seq_copy(src, dst, send, recv, peer):
    return pltpu.make_async_remote_copy(
        src_ref=src, dst_ref=dst, send_sem=send, recv_sem=recv,
        device_id={"seq": peer}, device_id_type=MESH,
    )


def tp_copy(src, dst, send, recv, peer):
    return pltpu.make_async_remote_copy(
        src_ref=src, dst_ref=dst, send_sem=send, recv_sem=recv,
        device_id={"tp": peer}, device_id_type=MESH,
    )


def greet(ranks, parts, me, tp):
    barrier = pltpu.get_barrier_semaphore()
    for d in range(1, ranks):
        pl.semaphore_signal(barrier, inc=1, device_id={"seq": lax.rem(me + d, ranks)}, device_id_type=MESH)
    for d in range(1, parts):
        pl.semaphore_signal(barrier, inc=1, device_id={"tp": lax.rem(tp + d, parts)}, device_id_type=MESH)
    pl.semaphore_wait(barrier, ranks + parts - 2)


class Gather:
    def __init__(self, full, rows, ranks, line, me, send_z, recv_z, send_x, recv_x):
        self.full, self.rows, self.line, self.long = full, rows, line, ranks // line
        self.z, self.x = me // line, lax.rem(me, line)
        self.sems = (send_z, recv_z, send_x, recv_x)

    def slot(self, z, x):
        return self.full.at[pl.ds(pl.multiple_of((z * self.line + x) * self.rows, self.rows), self.rows)]

    def along(self, way, k):
        sign = 1 if way == 0 else -1
        block = self.slot(self.z - sign * (k - 1), self.x)
        return seq_copy(block, block, self.sems[0].at[way, k], self.sems[1].at[way, k],
                        (self.z + sign) * self.line + self.x)

    def sends(self, way, k):
        sign = 1 if way == 0 else -1
        there, origin = self.z + sign, self.z - sign * (k - 1)
        return (there >= 0) & (there < self.long) & (origin >= 0) & (origin < self.long)

    def comes(self, way, k):
        origin = self.z - (1 if way == 0 else -1) * k
        return (origin >= 0) & (origin < self.long)

    def beside(self, d, z):
        block = self.slot(z, self.x)
        return seq_copy(block, block, self.sems[2].at[d, z], self.sems[3].at[d, z],
                        self.z * self.line + lax.rem(self.x + d, self.line))

    def start(self):
        for way in range(2):
            @pl.when(self.sends(way, 1))
            def _():
                self.along(way, 1).start()
        for d in range(1, self.line):
            self.beside(d, self.z).start()

    def step(self, k):
        for way in range(2):
            @pl.when(self.comes(way, k))
            def _():
                origin = self.z - (1 if way == 0 else -1) * k
                arrived = self.slot(origin, self.x)
                seq_copy(arrived, arrived, self.sems[0].at[way, k], self.sems[1].at[way, k],
                         lax.rem(self.z + 1, self.long) * self.line + self.x).wait_recv()
                if k + 1 < self.long:
                    @pl.when(self.sends(way, k + 1))
                    def _():
                        self.along(way, k + 1).start()
                for d in range(1, self.line):
                    self.beside(d, origin).start()

    def finish(self):
        for way in range(2):
            for k in range(1, self.long):
                @pl.when(self.sends(way, k))
                def _():
                    self.along(way, k).wait_send()
        for d in range(1, self.line):
            for z in range(self.long):
                self.beside(d, z).wait_send()
                arrived = self.slot(z, lax.rem(self.x + self.line - d, self.line))
                seq_copy(arrived, arrived, self.sems[2].at[d, z], self.sems[3].at[d, z],
                         self.z * self.line + lax.rem(self.x + d, self.line)).wait_recv()


def gather_sems(ranks, line):
    long = ranks // line
    return [pltpu.SemaphoreType.DMA((2, long))] * 2 + [pltpu.SemaphoreType.DMA((max(line, 2), long))] * 2


CHUNKS = 4


def tp_sum(part, pair, chip, chips, total, send, recv, parts, tp):
    across = parts // 2
    core, y = lax.rem(tp, 2), tp // 2
    sibling = y * 2 + (1 - core)
    wide = part.shape[1] // 2
    rows = part.shape[0] // CHUNKS
    mine = pl.ds(pl.multiple_of(core * wide, wide), wide)
    theirs = pl.ds(pl.multiple_of((1 - core) * wide, wide), wide)

    def first(n):
        at = pl.ds(n * rows, rows)
        return tp_copy(part.at[at, theirs], pair.at[at], send.at[0, n], recv.at[0, n], sibling)

    def second(d, n):
        at = pl.ds(n * rows, rows)
        return tp_copy(chip.at[at], chips.at[d, at], send.at[d, n], recv.at[d, n], lax.rem(y + d, across) * 2 + core)

    def third(n):
        at = pl.ds(n * rows, rows)
        return tp_copy(total.at[at, mine], total.at[at, mine], send.at[across, n], recv.at[across, n], sibling)

    def third_in(n):
        at = pl.ds(n * rows, rows)
        return tp_copy(total.at[at, theirs], total.at[at, theirs], send.at[across, n], recv.at[across, n], sibling)

    for n in range(CHUNKS):
        first(n).start()
    for n in range(CHUNKS):
        at = pl.ds(n * rows, rows)
        first(n).wait_recv()
        chip[at, :] = (part[at, mine].astype(F32) + pair[at, :].astype(F32)).astype(BF)
        for d in range(1, across):
            second(d, n).start()
    for n in range(CHUNKS):
        at = pl.ds(n * rows, rows)
        whole = chip[at, :].astype(F32)
        for d in range(1, across):
            second(d, n).wait_recv()
            whole = whole + chips[d, at, :].astype(F32)
        total[at, mine] = whole.astype(BF)
        third(n).start()
    for n in range(CHUNKS):
        third_in(n).wait_recv()
    for n in range(CHUNKS):
        first(n).wait_send()
        third(n).wait_send()
        for d in range(1, across):
            second(d, n).wait_send()


def tp_sum_scratch(tokens, width, parts):
    across = parts // 2
    return [
        pltpu.VMEM((tokens, width // 2), BF),
        pltpu.VMEM((tokens, width // 2), BF),
        pltpu.VMEM((across, tokens, width // 2), BF),
        pltpu.SemaphoreType.DMA((across + 1, CHUNKS)),
        pltpu.SemaphoreType.DMA((across + 1, CHUNKS)),
    ]


def iotas(size):
    return lax.broadcasted_iota(jnp.int32, (size, size), 0), lax.broadcasted_iota(jnp.int32, (size, size), 1)


def decays(decay, beta, size):
    rows, cols = iotas(size)
    log_decay = -0.5 * jnp.exp(-LOG_TWO * decay.astype(F32))
    spread_out = jnp.broadcast_to(log_decay, (size, size))
    total_row = jnp.sum(jnp.where(rows <= cols, spread_out, 0.0), axis=0, keepdims=True)
    total_col = jnp.sum(jnp.where(cols <= rows, spread_out.T, 0.0), axis=1, keepdims=True)
    up_to = rows >= cols
    factors = jnp.where(up_to, jnp.exp(jnp.where(up_to, total_col - total_row, 0.0)), 0.0)
    final = total_col[size - 1 :, :]
    rate = (beta.astype(F32) + 1.0) / 8.0
    return jnp.exp(total_col), jnp.exp(final - total_col), jnp.exp(final), factors, rate


def convolved(ext_ref, taps, b, at, width, tokens):
    return sum(
        taps[j : j + 1, :] * ext_ref[b, pl.ds(HALO - CONV + 1 + j, tokens), pl.ds(at, width)] for j in range(CONV)
    )


def unit_inverses(strict, size):
    rows, cols = iotas(size)

    def below(k):
        return ((rows >> (k + 1)) == (cols >> (k + 1))) & (((rows >> k) & 1) == 1) & (((cols >> k) & 1) == 0)

    eye = (rows == cols).astype(F32)
    found = [eye - jnp.where(below(0), a, 0.0) for a in strict]
    for k in range(1, size.bit_length() - 1):
        moved = [mm3(jnp.where(below(k), a, 0.0), x) for a, x in zip(strict, found)]
        found = [x - mm3(x, m) for x, m in zip(found, moved)]
    return found


def forward_kernel(
    dims, x_in, cot_in, wq, wk, wv, wo, out_in, ffn_in, small_in, decay, beta,
    first, out_t, ffn, x_full, cot_full, small, normed, ext, gate_pre, mixed, gated, attn, start, trans, reach,
    smalls, local, chain_in, chain_out, attn_part, pair, chip, chips,
    small_send, small_recv, tok_send, tok_recv, halo_sems, chain_send, chain_recv, sum_send, sum_recv, *gather,
):
    ranks, parts, line, seqs, tokens, heads = dims
    me, tp = lax.axis_index("seq"), lax.axis_index("tp")
    long = ranks // line
    rows = wq.shape[0]
    q_wide, v_wide = wq.shape[1], wv.shape[1]
    qkv_wide = 2 * q_wide + v_wide
    greet(ranks, parts, me, tp)
    one = Gather(first, rows, ranks, line, me, *gather[0:4])
    two = Gather(out_t, rows, ranks, line, me, *gather[4:8])
    three = Gather(ffn, rows, ranks, line, me, *gather[8:12])

    part_wide = x_in.shape[1]
    own = pl.ds(pl.multiple_of(tp * part_wide, part_wide), part_wide)

    def token_copy(which, src, dst, d):
        return tp_copy(src, dst.at[:, own], tok_send.at[which, d], tok_recv.at[which, d], lax.rem(tp + d, parts))

    def token_wait(which, src, dst, d):
        tp_copy(src, dst.at[:, pl.ds(pl.multiple_of(lax.rem(tp + parts - d, parts) * part_wide, part_wide), part_wide)],
                tok_send.at[which, d], tok_recv.at[which, d], lax.rem(tp + d, parts)).wait_recv()

    def small_copy(d):
        return seq_copy(small_in, smalls.at[d], small_send.at[d], small_recv.at[d], lax.rem(me + d, ranks))

    for d in range(1, parts):
        token_copy(0, x_in, x_full, d).start()
    for d in range(1, ranks):
        small_copy(d).start()
    here = pl.ds(pl.multiple_of(me * rows, rows), rows)
    first[here, 0:q_wide] = wq[...]
    first[here, q_wide : 2 * q_wide] = wk[...]
    first[here, 2 * q_wide : qkv_wide] = wv[...]
    first[here, qkv_wide:] = wo[...]
    one.start()
    out_t[here, :] = out_in[...]
    ffn[here, :] = ffn_in[...]
    for d in range(1, parts):
        token_copy(1, cot_in, cot_full, d).start()
    x_full[:, own] = x_in[...]
    cot_full[:, own] = cot_in[...]

    total = small_in[...].astype(F32)
    for d in range(1, ranks):
        small_copy(d).wait_recv()
        total = total + smalls[d].astype(F32)
    small[...] = total
    for d in range(1, parts):
        token_wait(0, x_in, x_full, d)
    residual = x_full[...].astype(F32)
    scale = lax.rsqrt(jnp.mean(residual * residual, axis=-1, keepdims=True) + EPSILON)
    normed[...] = (residual * scale * small[0:1, 0 : residual.shape[1]]).astype(BF)

    sequence_heads = [(b, h) for b in range(seqs) for h in range(heads)]
    for k in range(1, long):
        one.step(k)
    one.finish()
    two.start()
    tile = 256

    def project(n, carry):
        cols = pl.ds(pl.multiple_of(n * tile, tile), tile)
        found = mm(normed[...], first[:, cols])
        for b in range(seqs):
            ext[b, pl.ds(HALO, tokens), cols] = found[b * tokens : (b + 1) * tokens]
        return carry

    lax.fori_loop(0, qkv_wide // tile, project, 0)

    halo = seq_copy(ext.at[:, pl.ds(tokens, HALO)], ext.at[:, pl.ds(0, HALO)], halo_sems.at[0], halo_sems.at[1],
                    lax.rem(me + 1, ranks))

    @pl.when(me < ranks - 1)
    def _():
        halo.start()

    @pl.when(me == 0)
    def _():
        ext[:, 0:HALO, :] = jnp.zeros((seqs, HALO, qkv_wide), F32)

    def project_gate(n, carry):
        cols = pl.ds(pl.multiple_of(n * tile, tile), tile)
        gate_pre[:, cols] = mm(normed[...], first[:, pl.ds(pl.multiple_of(qkv_wide + n * tile, tile), tile)])
        return carry

    lax.fori_loop(0, v_wide // tile, project_gate, 0)

    @pl.when(me > 0)
    def _():
        halo.wait_recv()

    two.step(1)

    rows_i, cols_i = iotas(tokens)
    state = []
    for b, h in sequence_heads:
        taps = small[2:6, :]
        q_at, k_at, v_at = h * DK, q_wide + h * DK, 2 * q_wide + h * DV
        growth, fade, kept, factors, rate = decays(
            decay[pl.ds(b * tokens, tokens), h : h + 1], beta[pl.ds(b * tokens, tokens), h : h + 1], tokens
        )
        query = convolved(ext, taps[:, q_at : q_at + DK], b, q_at, DK, tokens)
        query = query * sigmoid(query)
        query = query * (lax.rsqrt(jnp.sum(query * query, axis=-1, keepdims=True) + EPSILON) * DK**-0.5)
        keys = convolved(ext, taps[:, k_at : k_at + DK], b, k_at, DK, tokens)
        keys = keys * sigmoid(keys)
        keys = keys * lax.rsqrt(jnp.sum(keys * keys, axis=-1, keepdims=True) + EPSILON)
        values = convolved(ext, taps[:, v_at : v_at + DV], b, v_at, DV, tokens)
        values = values * sigmoid(values)
        strict = jnp.where(rows_i > cols_i, rate * mm3(keys, keys, NT) * factors, 0.0)
        scores = mm3(query, keys, NT) * factors
        state.append((growth, fade, kept, rate, query, keys, values, strict, scores))
    inverses = unit_inverses([s[7] for s in state], tokens)
    for n, (growth, fade, kept, rate, query, keys, values, strict, scores) in enumerate(state):
        inverse = inverses[n]
        written = mm3(inverse, rate * values)
        erased = mm3(inverse, (rate * growth) * keys)
        faded = keys * fade
        reach[n] = growth * query - mm3(scores, erased)
        b, h = sequence_heads[n]
        mixed[pl.ds(b * tokens, tokens), h * DV : (h + 1) * DV] = mm3(scores, written)
        trans[n] = jnp.where(rows_i == cols_i, kept, 0.0) - mm3(faded, erased, TN)
        local[n] = mm3(faded, written, TN)

    for k in range(2, long):
        two.step(k)
    two.finish()
    three.start()

    def chain_copy(n):
        return seq_copy(chain_out.at[n], chain_in.at[n], chain_send.at[n], chain_recv.at[n], lax.rem(me + 1, ranks))

    for n in range(len(sequence_heads)):
        @pl.when(me > 0)
        def _():
            chain_copy(n).wait_recv()
            start[n] = chain_in[n]

        @pl.when(me == 0)
        def _():
            start[n] = jnp.zeros((DK, DV), BF)

        @pl.when(me < ranks - 1)
        def _():
            chain_out[n] = (mm2(trans[n], start[n]) + local[n]).astype(BF)
            chain_copy(n).start()

    for n, (b, h) in enumerate(sequence_heads):
        at, cols = pl.ds(b * tokens, tokens), pl.ds(h * DV, DV)
        whole = mixed[at, cols] + mm2(reach[n], start[n])
        mixed[at, cols] = whole
        scale = lax.rsqrt(jnp.mean(whole * whole, axis=-1, keepdims=True) + EPSILON)
        pre = gate_pre[at, cols]
        gated[at, cols] = (whole * scale * small[6:7, cols] * (pre * sigmoid(pre))).astype(BF)

    def give_out(n, carry):
        cols = pl.ds(pl.multiple_of(n * tile, tile), tile)
        attn_part[:, cols] = mm(gated[...], out_t[cols, :], NT).astype(BF)
        return carry

    lax.fori_loop(0, attn_part.shape[1] // tile, give_out, 0)
    tp_sum(attn_part, pair, chip, chips, attn, sum_send, sum_recv, parts, tp)

    for k in range(1, long):
        three.step(k)
    three.finish()
    for d in range(1, parts):
        token_wait(1, cot_in, cot_full, d)
        token_copy(0, x_in, x_full, d).wait_send()
        token_copy(1, cot_in, cot_full, d).wait_send()
    for d in range(1, ranks):
        small_copy(d).wait_send()

    @pl.when(me < ranks - 1)
    def _():
        halo.wait_send()
        for n in range(len(sequence_heads)):
            chain_copy(n).wait_send()


def forward_call(dims, x_in, cot_in, wq, wk, wv, wo, out_in, ffn_in, small_in, decay, beta):
    ranks, parts, line, seqs, tokens, heads = dims
    count = seqs * heads
    all_tokens = seqs * tokens
    width = wq.shape[0] * ranks
    rows = wq.shape[0]
    first_wide = wq.shape[1] * 2 + wv.shape[1] * 2
    qkv_wide = wq.shape[1] * 2 + wv.shape[1]
    v_wide = wv.shape[1]
    s = jax.ShapeDtypeStruct
    outs = [
        s((width, first_wide), BF), s((width, out_in.shape[1]), BF), s((width, ffn_in.shape[1]), BF),
        s((all_tokens, width), BF), s((all_tokens, width), BF), s(small_in.shape, F32), s((all_tokens, width), BF),
        s((seqs, HALO + tokens, qkv_wide), F32), s((all_tokens, v_wide), F32), s((all_tokens, v_wide), F32),
        s((all_tokens, v_wide), BF), s((all_tokens, width), BF), s((count, DK, DV), BF), s((count, DK, DK), F32),
        s((count, tokens, DK), F32),
    ]
    vmem = pl.BlockSpec(memory_space=pltpu.VMEM)
    dma = pltpu.SemaphoreType.DMA
    scratch = [
        pltpu.VMEM((ranks,) + small_in.shape, BF), pltpu.VMEM((count, DK, DV), F32), pltpu.VMEM((count, DK, DV), BF),
        pltpu.VMEM((count, DK, DV), BF), pltpu.VMEM((all_tokens, width), BF),
    ]
    sums = tp_sum_scratch(all_tokens, width, parts)
    scratch += sums[:3] + [dma((ranks,)), dma((ranks,)), dma((2, parts)), dma((2, parts)), dma((2,)), dma((count,)),
                           dma((count,))] + sums[3:]
    scratch += gather_sems(ranks, line) * 3
    return pl.pallas_call(
        functools.partial(forward_kernel, dims),
        out_shape=outs,
        in_specs=[vmem] * 11,
        out_specs=[vmem] * len(outs),
        scratch_shapes=scratch,
        compiler_params=pltpu.CompilerParams(collective_id=0, has_side_effects=True, vmem_limit_bytes=44 * 2**20),
        name="forward",
    )(x_in, cot_in, wq, wk, wv, wo, out_in, ffn_in, small_in, decay, beta)


D = 1024
BLOCK = 64
PRECISE = lax.Precision.HIGHEST
SPLIT = lax.Precision.HIGH


def shifted(block, axis, distance):
    devices = range(lax.axis_size(axis))
    route = [(i - distance, i) for i in devices if i - distance in devices]
    return lax.ppermute(block, axis, route)


def before_me(joint, axis):
    size = lax.axis_size(axis)
    held = shifted(joint.astype(jnp.bfloat16), axis, 1).astype(jnp.float32)
    distance = 1
    while distance < size:
        last = 2 * distance >= size
        sent = held[..., DK:] if last else held
        got = shifted(sent.astype(jnp.bfloat16), axis, distance).astype(jnp.float32)
        moved = jnp.matmul(held[..., :DK], got, precision=PRECISE)
        if last:
            return held[..., DK:] + moved
        held = jnp.concatenate(
            [moved[..., :DK], held[..., DK:] + moved[..., DK:]], axis=-1
        )
        distance *= 2
    return held[..., DK:]


def later_maps(transition, axis):
    size = lax.axis_size(axis)
    held = shifted(transition.astype(jnp.bfloat16), axis, -1).astype(jnp.float32)
    maps = [held]
    distance = 1
    while 2 * distance < size:
        got = shifted(held.astype(jnp.bfloat16), axis, -distance).astype(jnp.float32)
        held = jnp.matmul(got, held, precision=PRECISE)
        maps.append(held)
        distance *= 2
    return maps


def after_me(d_start, maps, axis):
    size = lax.axis_size(axis)
    held = shifted(d_start.astype(jnp.bfloat16), axis, -1).astype(jnp.float32)
    distance = 1
    for step in maps:
        if distance >= size:
            break
        got = shifted(held.astype(jnp.bfloat16), axis, -distance).astype(jnp.float32)
        held = held + jnp.einsum("bhkj,bhkw->bhjw", step, got, precision=PRECISE)
        distance *= 2
    return held


def row_scale(values):
    return lax.rsqrt(jnp.mean(values * values, axis=-1, keepdims=True) + EPSILON)


def silu_slope(values):
    sigmoid = jax.nn.sigmoid(values)
    return sigmoid * (1.0 + values * (1.0 - sigmoid))


def norm_back(d_normed, inputs, scales, gains):
    weighted = d_normed * gains
    return scales * (
        weighted - inputs * scales * scales * jnp.mean(weighted * inputs, axis=-1, keepdims=True)
    )


@jax.custom_vjp
def unit_inverse(strict_part):
    width = strict_part.shape[-1]
    negated = -strict_part
    result = jnp.eye(width, dtype=strict_part.dtype) + negated
    for rounds in range(width.bit_length() - 2):
        negated = jnp.matmul(negated, negated, precision=PRECISE)
        result = result + jnp.matmul(result, negated, precision=PRECISE)
    return result


def unit_inverse_forward(strict_part):
    result = unit_inverse(strict_part)
    return result, result


def unit_inverse_backward(result, d_result):
    flipped = jnp.swapaxes(result, -1, -2)
    inner = jnp.matmul(d_result, flipped, precision=SPLIT)
    return (-jnp.matmul(flipped, inner, precision=SPLIT),)


unit_inverse.defvjp(unit_inverse_forward, unit_inverse_backward)


def delta_run(state_in, query, keys, values, log_decay, write_strength_rate):
    leading = query.shape[:-2]
    length = query.shape[-2]
    blocks = length // BLOCK
    axis_at = len(leading)

    def split_blocks(tensor):
        return tensor.reshape(leading + (blocks, BLOCK) + tensor.shape[axis_at + 1 :])

    query, keys, values, log_decay, rate = (
        split_blocks(a) for a in (query, keys, values, log_decay, write_strength_rate)
    )
    locations = jnp.arange(BLOCK)
    no_later = locations[:, None] >= locations[None, :]
    cumulative = jnp.sum(jnp.where(no_later, log_decay[..., None, :], 0.0), axis=-1)
    strictly = (locations[:, None] > locations[None, :]).astype(state_in.dtype)
    up_to = locations[:, None] >= locations[None, :]
    spread = cumulative[..., :, None] - cumulative[..., None, :]
    factors = jnp.exp(jnp.where(up_to, spread, 0.0)) * up_to.astype(state_in.dtype)
    key_dots = jnp.einsum("...td,...sd->...ts", keys, keys, precision=SPLIT)
    inverse = unit_inverse(rate[..., :, None] * key_dots * factors * strictly)
    growth = jnp.exp(cumulative)
    written = jnp.matmul(inverse, rate[..., None] * values, precision=SPLIT)
    erased = jnp.matmul(inverse, (rate * growth)[..., None] * keys, precision=SPLIT)
    scores = jnp.einsum("...td,...sd->...ts", query, keys, precision=SPLIT) * factors
    grown = growth[..., None] * query
    final_log = cumulative[..., -1:]
    faded = keys * jnp.exp(final_log - cumulative)[..., None]
    kept = jnp.exp(final_log)[..., None]
    state, outputs = state_in, []
    for block in range(blocks):
        at = (slice(None),) * axis_at + (block,)
        update = written[at] - jnp.matmul(erased[at], state, precision=SPLIT)
        outputs.append(
            jnp.matmul(grown[at], state, precision=SPLIT)
            + jnp.matmul(scores[at], update, precision=SPLIT)
        )
        state = kept[at] * state + jnp.einsum(
            "...sd,...sw->...dw", faded[at], update, precision=SPLIT
        )
    outputs = jnp.concatenate(outputs, axis=axis_at)
    return (outputs, state)


def conv_valid(kernel, extended):
    length = extended.shape[1] - kernel.shape[0] + 1
    return sum(
        (
            kernel[offset] * extended[:, offset : offset + length]
            for offset in range(kernel.shape[0])
        )
    )


def heads_first(tensor, width):
    shaped = tensor.reshape(tensor.shape[0], tensor.shape[1], -1, width)
    return jnp.transpose(shaped, (0, 2, 1, 3))


def rows_last(tensor):
    shaped = jnp.transpose(tensor, (0, 2, 1, 3))
    return shaped.reshape(shaped.shape[0], shaped.shape[1], -1)


def activate(kern_query, kern_key, kern_value, ext_query, ext_key, ext_value):
    query = heads_first(jax.nn.silu(conv_valid(kern_query, ext_query)), DK)
    query = (
        query * lax.rsqrt(jnp.sum(query * query, axis=-1, keepdims=True) + EPSILON) * DK ** (-0.5)
    )
    keys = heads_first(jax.nn.silu(conv_valid(kern_key, ext_key)), DK)
    keys = keys * lax.rsqrt(jnp.sum(keys * keys, axis=-1, keepdims=True) + EPSILON)
    values = heads_first(jax.nn.silu(conv_valid(kern_value, ext_value)), DV)
    return (query, keys, values)


def gate_rates(decay_code, beta_code):
    log_decay = -0.5 * jnp.exp(-LOG_TWO * decay_code.astype(jnp.float32))
    write_strength_rate = (beta_code.astype(jnp.float32) + 1.0) / 8.0
    return (jnp.moveaxis(log_decay, 2, 1), jnp.moveaxis(write_strength_rate, 2, 1))


def fold_edge(tensor, incoming):
    margin = incoming.shape[1]
    return jnp.concatenate([tensor[:, :-margin], tensor[:, -margin:] + incoming], axis=1)


def per_device(
    line,
    block_in,
    out_grad,
    decay_code,
    beta_code,
    norm_gain,
    w_query,
    w_key,
    w_value,
    w_outgate,
    conv_query,
    conv_key,
    conv_value,
    head_gain,
    w_output,
    mlp_gain,
    w_gate,
    w_up,
    w_down,
):
    seq_count, tok_count, width_part = block_in.shape
    heads_here = decay_code.shape[2]
    ranks = lax.axis_size("seq")
    parts = lax.axis_size("tp")
    smalls = (norm_gain, mlp_gain, conv_query, conv_key, conv_value, head_gain)
    flat_size = sum(a.size for a in smalls)
    extra = -(-flat_size // norm_gain.shape[0])
    widths = (w_query.shape[1], w_key.shape[1], w_value.shape[1], w_outgate.shape[1])
    mixer_width = sum(widths)
    hidden_width = w_gate.shape[1]
    out_width = w_output.shape[0]
    mine = jnp.arange(ranks) == lax.axis_index("seq")

    def place(a, lead):
        a = jnp.where(mine[:, None], a.reshape(-1, 1, a.shape[-1]), 0)
        return a.reshape(lead, -1)

    small_wide = max(norm_gain.shape[0] * ranks, heads_here * (2 * DK + DV))

    def row(a):
        return jnp.pad(a, ((0, 0), (0, small_wide - a.shape[1])))

    packed = jnp.concatenate(
        [
            row(place(norm_gain, 1)),
            row(place(mlp_gain, 1)),
            row(jnp.concatenate([place(a, CONV) for a in (conv_query, conv_key, conv_value)], axis=1)),
            row(place(head_gain, 1)),
            jnp.zeros((SMALL_ROWS - 3 - CONV, small_wide), jnp.bfloat16),
        ],
        axis=0,
    )
    dims = (ranks, parts, line, seq_count, tok_count, heads_here)
    (full_mixer, output_t, full_ffn, input_full, cot_full, small, normed, ext, gate_flat, mixed_flat, gated, attn, start,
     transition, reach) = forward_call(
        dims, block_in.reshape(-1, width_part), out_grad.reshape(-1, width_part), w_query, w_key, w_value, w_outgate,
        w_output.T, jnp.concatenate([w_gate, w_up, w_down.T], axis=1), packed,
        decay_code.reshape(-1, heads_here), beta_code.reshape(-1, heads_here),
    )
    full_gate_up = full_ffn[:, : 2 * hidden_width]
    down_t = full_ffn[:, 2 * hidden_width :]
    model = input_full.shape[1]
    gain_one, gain_two = small[0, :model], small[1, :model]
    cuts = (widths[0], widths[0] + widths[1], widths[0] + widths[1] + widths[2])
    gain_head = small[2 + CONV, : widths[2]].reshape(1, heads_here, 1, DV)
    taps = small[2 : 2 + CONV]
    kernels = (taps[:, : cuts[0]], taps[:, cuts[0] : cuts[1]], taps[:, cuts[1] : cuts[2]])
    residual = input_full.astype(jnp.float32)
    scale_one = row_scale(residual)
    margin = CONV - 1
    ext_qkv = ext[:, HALO - margin :]
    ext_query, ext_key, ext_value = (
        ext_qkv[..., : cuts[0]],
        ext_qkv[..., cuts[0] : cuts[1]],
        ext_qkv[..., cuts[1] :],
    )
    log_decay, write_strength_rate = gate_rates(decay_code, beta_code)
    by_head = lambda a: a.reshape((seq_count, heads_here) + a.shape[1:])
    start_state = by_head(start).astype(jnp.float32)
    maps = later_maps(by_head(transition), "seq")
    start_map = by_head(reach)
    mixed = heads_first(mixed_flat.reshape(seq_count, tok_count, -1), DV)
    head_scale = row_scale(mixed)
    head_out = mixed * head_scale * gain_head
    gate_pre = heads_first(gate_flat.reshape(seq_count, tok_count, -1), DV)
    attn = attn.astype(jnp.float32)
    middle = residual + attn
    tp_at = lax.axis_index("tp") * width_part
    mid_part = lax.dynamic_slice_in_dim(middle, tp_at, width_part, 1).reshape(
        seq_count, tok_count, width_part
    )
    scale_two = row_scale(middle)
    normed_two = (middle * scale_two * gain_two).astype(jnp.bfloat16)
    pre_both = jnp.dot(normed_two, full_gate_up, preferred_element_type=jnp.float32)
    pre_gate, pre_up = pre_both[:, :hidden_width], pre_both[:, hidden_width:]
    hidden = (jax.nn.silu(pre_gate) * pre_up).astype(jnp.bfloat16)
    feedforward_portion = jnp.einsum(
        "tk,nk->tn", hidden, down_t, preferred_element_type=jnp.float32
    ).reshape(seq_count, tok_count, D)
    fed = lax.psum_scatter(
        feedforward_portion.astype(jnp.bfloat16), "tp", scatter_dimension=2, tiled=True
    )
    cotangent = cot_full
    d_hidden = jnp.dot(cotangent, down_t, preferred_element_type=jnp.float32)
    grad_down_t = jnp.dot(cotangent.T, hidden, preferred_element_type=jnp.float32)
    d_pre_gate = (d_hidden * pre_up * silu_slope(pre_gate)).astype(jnp.bfloat16)
    d_pre_up = (d_hidden * jax.nn.silu(pre_gate)).astype(jnp.bfloat16)
    d_pre_both = jnp.concatenate([d_pre_gate, d_pre_up], axis=1)
    d_two_part = jnp.einsum(
        "tk,nk->tn", d_pre_both, full_gate_up, preferred_element_type=jnp.float32
    )
    d_normed_two = lax.psum(d_two_part.astype(jnp.bfloat16), "tp").astype(jnp.float32)
    grad_gate_up = jnp.dot(normed_two.T, d_pre_both, preferred_element_type=jnp.float32)
    grad_mlp_gain = jnp.sum(d_normed_two * middle * scale_two, axis=0)
    d_middle = cotangent.astype(jnp.float32) + norm_back(d_normed_two, middle, scale_two, gain_two)
    d_mid_low = d_middle.astype(jnp.bfloat16)
    d_gated = jnp.dot(d_mid_low, output_t, preferred_element_type=jnp.float32)
    grad_output_t = jnp.dot(d_mid_low.T, gated, preferred_element_type=jnp.float32)
    late = lax.psum_scatter(
        jnp.concatenate(
            [
                grad_gate_up.astype(jnp.bfloat16),
                grad_output_t.astype(jnp.bfloat16),
                grad_down_t.astype(jnp.bfloat16),
            ],
            axis=1,
        ),
        "seq",
        scatter_dimension=0,
        tiled=True,
    )
    d_gated_heads = heads_first(d_gated.reshape(seq_count, tok_count, -1), DV)
    d_outgate = (
        rows_last(d_gated_heads * head_out * silu_slope(gate_pre))
        .reshape(seq_count * tok_count, -1)
        .astype(jnp.bfloat16)
    )
    d_head = d_gated_heads * jax.nn.silu(gate_pre)
    grad_head_gain = jnp.sum(d_head * mixed * head_scale, axis=(0, 2))
    d_mixed = norm_back(d_head, mixed, head_scale, gain_head)
    d_start = jnp.einsum("bhtk,bhtw->bhkw", start_map, d_mixed, precision=PRECISE)
    d_end = after_me(d_start, maps, "seq")

    def mixer(kern_q, kern_k, kern_v, ext_q, ext_k, ext_v, start_in):
        query_in, keys_in, values_in = activate(kern_q, kern_k, kern_v, ext_q, ext_k, ext_v)
        return delta_run(start_in, query_in, keys_in, values_in, log_decay, write_strength_rate)

    mixer_out, mixer_back = jax.vjp(
        mixer, kernels[0], kernels[1], kernels[2], ext_query, ext_key, ext_value, start_state
    )
    totals = mixer_back((d_mixed, d_end))
    d_ext = jnp.concatenate([totals[3], totals[4], totals[5]], axis=-1)
    after = shifted(d_ext[:, :margin], "seq", -1)
    d_proj = fold_edge(d_ext[:, margin:], after).reshape(seq_count * tok_count, -1)
    d_proj = jnp.concatenate([d_proj.astype(jnp.bfloat16), d_outgate], axis=1)
    d_normed_part = jnp.einsum("tk,nk->tn", d_proj, full_mixer, preferred_element_type=jnp.float32)
    grad_mixer = jnp.dot(normed.T, d_proj, preferred_element_type=jnp.float32)
    d_normed_part, fed, late = lax.optimization_barrier((d_normed_part, fed, late))
    late = late.astype(jnp.float32)
    block_out = (mid_part + fed.astype(jnp.float32)).astype(jnp.bfloat16)
    d_normed = (
        lax.psum(d_normed_part.reshape(seq_count, tok_count, D).astype(jnp.bfloat16), "tp")
        .astype(jnp.float32)
        .reshape(-1, D)
    )
    grad_norm_gain = jnp.sum(d_normed * residual * scale_one, axis=0)
    grad_full = (d_middle + norm_back(d_normed, residual, scale_one, gain_one)).reshape(
        seq_count, tok_count, D
    )
    grad_in = lax.dynamic_slice_in_dim(grad_full, lax.axis_index("tp") * width_part, width_part, 2)
    conv_grads = tuple(
        jnp.moveaxis(total.reshape(CONV, heads_here, ranks, -1), 2, 0).reshape(ranks, -1)
        for total in totals[:3]
    )
    small_grads = jnp.concatenate(
        [
            grad_norm_gain.reshape(ranks, -1),
            grad_mlp_gain.reshape(ranks, -1),
            *conv_grads,
            jnp.moveaxis(grad_head_gain.reshape(heads_here, ranks, -1), 1, 0).reshape(ranks, -1),
        ],
        axis=1,
    )
    small_grads = jnp.pad(
        small_grads, ((0, 0), (0, extra * norm_gain.shape[0] - small_grads.shape[1]))
    ).reshape(ranks * norm_gain.shape[0], extra)
    final = lax.psum_scatter(
        jnp.concatenate(
            [grad_mixer.astype(jnp.bfloat16), small_grads.astype(jnp.bfloat16)], axis=1
        ),
        "seq",
        scatter_dimension=0,
        tiled=True,
    ).astype(jnp.float32)
    small_here = final[:, mixer_width:].reshape(-1)
    small_out, at = [], 0
    for a in smalls:
        small_out.append(small_here[at : at + a.size].reshape(a.shape))
        at += a.size
    return (
        block_out,
        grad_in,
        small_out[0],
        final[:, : cuts[0]],
        final[:, cuts[0] : cuts[1]],
        final[:, cuts[1] : cuts[2]],
        final[:, cuts[2] : mixer_width],
        small_out[2],
        small_out[3],
        small_out[4],
        small_out[5],
        late[:, 2 * hidden_width : 2 * hidden_width + out_width].T,
        small_out[1],
        late[:, :hidden_width],
        late[:, hidden_width : 2 * hidden_width],
        late[:, 2 * hidden_width + out_width :].T,
    )


def solution(mesh):
    spots = [getattr(d, "coords", (0, 0, 0)) for d in mesh.devices[:, 0]]
    line = max(1, len({spot[0] for spot in spots}))
    if mesh.shape["seq"] % line:
        line = 1
    return jax.shard_map(
        functools.partial(per_device, line),
        mesh=mesh,
        in_specs=(
            P(None, "seq", "tp"),
            P(None, "seq", "tp"),
            P(None, "seq", "tp"),
            P(None, "seq", "tp"),
            P("seq"),
            P("seq", "tp"),
            P("seq", "tp"),
            P("seq", "tp"),
            P("seq", "tp"),
            P(None, "tp", "seq"),
            P(None, "tp", "seq"),
            P(None, "tp", "seq"),
            P("tp", "seq"),
            P("tp", "seq"),
            P("seq"),
            P("seq", "tp"),
            P("seq", "tp"),
            P("tp", "seq"),
        ),
        out_specs=(
            P(None, "seq", "tp"),
            P(None, "seq", "tp"),
            P("seq"),
            P("seq", "tp"),
            P("seq", "tp"),
            P("seq", "tp"),
            P("seq", "tp"),
            P(None, "tp", "seq"),
            P(None, "tp", "seq"),
            P(None, "tp", "seq"),
            P("tp", "seq"),
            P("tp", "seq"),
            P("seq"),
            P("seq", "tp"),
            P("seq", "tp"),
            P("tp", "seq"),
        ),
        check_vma=False,
    )
```

```python
import functools

import jax
import jax.numpy as jnp
from jax import lax
from jax.experimental import pallas as pl
from jax.experimental.pallas import tpu as pltpu
from jax.sharding import PartitionSpec as P

DK = 128
DV = 256
CONV = 4
HALO = 8
SMALL_ROWS = 16
EPSILON = 1e-06
LOG_TWO = 0.6931471805599453
MESH = pl.DeviceIdType.MESH
NN = ((1,), (0,))
NT = ((1,), (1,))
TN = ((0,), (0,))
BF = jnp.bfloat16
F32 = jnp.float32


def mm(a, b, dims=NN):
    return lax.dot_general(a, b, (dims, ((), ())), preferred_element_type=F32)


def halves(a):
    high = a.astype(BF)
    return high, (a - high.astype(F32)).astype(BF)


def mm3(a, b, dims=NN):
    a_high, a_low = halves(a)
    b_high, b_low = halves(b)
    return mm(a_high, b_high, dims) + (mm(a_high, b_low, dims) + mm(a_low, b_high, dims))


def mm2(a, b, dims=NN):
    a_high, a_low = halves(a)
    return mm(a_high, b, dims) + mm(a_low, b, dims)


def sigmoid(values):
    return 1.0 / (1.0 + jnp.exp(-values))


def seq_copy(src, dst, send, recv, peer):
    return pltpu.make_async_remote_copy(
        src_ref=src, dst_ref=dst, send_sem=send, recv_sem=recv,
        device_id={"seq": peer}, device_id_type=MESH,
    )


def tp_copy(src, dst, send, recv, peer):
    return pltpu.make_async_remote_copy(
        src_ref=src, dst_ref=dst, send_sem=send, recv_sem=recv,
        device_id={"tp": peer}, device_id_type=MESH,
    )


def greet(ranks, parts, me, tp):
    barrier = pltpu.get_barrier_semaphore()
    for d in range(1, ranks):
        pl.semaphore_signal(barrier, inc=1, device_id={"seq": lax.rem(me + d, ranks)}, device_id_type=MESH)
    for d in range(1, parts):
        pl.semaphore_signal(barrier, inc=1, device_id={"tp": lax.rem(tp + d, parts)}, device_id_type=MESH)
    pl.semaphore_wait(barrier, ranks + parts - 2)


class Gather:
    def __init__(self, full, rows, ranks, line, me, send_z, recv_z, send_x, recv_x):
        self.full, self.rows, self.line, self.long = full, rows, line, ranks // line
        self.z, self.x = me // line, lax.rem(me, line)
        self.sems = (send_z, recv_z, send_x, recv_x)

    def slot(self, z, x):
        return self.full.at[pl.ds(pl.multiple_of((z * self.line + x) * self.rows, self.rows), self.rows)]

    def along(self, way, k):
        sign = 1 if way == 0 else -1
        block = self.slot(self.z - sign * (k - 1), self.x)
        return seq_copy(block, block, self.sems[0].at[way, k], self.sems[1].at[way, k],
                        (self.z + sign) * self.line + self.x)

    def sends(self, way, k):
        sign = 1 if way == 0 else -1
        there, origin = self.z + sign, self.z - sign * (k - 1)
        return (there >= 0) & (there < self.long) & (origin >= 0) & (origin < self.long)

    def comes(self, way, k):
        origin = self.z - (1 if way == 0 else -1) * k
        return (origin >= 0) & (origin < self.long)

    def beside(self, d, z):
        block = self.slot(z, self.x)
        return seq_copy(block, block, self.sems[2].at[d, z], self.sems[3].at[d, z],
                        self.z * self.line + lax.rem(self.x + d, self.line))

    def start(self):
        for way in range(2):
            @pl.when(self.sends(way, 1))
            def _():
                self.along(way, 1).start()
        for d in range(1, self.line):
            self.beside(d, self.z).start()

    def step(self, k):
        for way in range(2):
            @pl.when(self.comes(way, k))
            def _():
                origin = self.z - (1 if way == 0 else -1) * k
                arrived = self.slot(origin, self.x)
                seq_copy(arrived, arrived, self.sems[0].at[way, k], self.sems[1].at[way, k],
                         lax.rem(self.z + 1, self.long) * self.line + self.x).wait_recv()
                if k + 1 < self.long:
                    @pl.when(self.sends(way, k + 1))
                    def _():
                        self.along(way, k + 1).start()
                for d in range(1, self.line):
                    self.beside(d, origin).start()

    def finish(self):
        for way in range(2):
            for k in range(1, self.long):
                @pl.when(self.sends(way, k))
                def _():
                    self.along(way, k).wait_send()
        for d in range(1, self.line):
            for z in range(self.long):
                self.beside(d, z).wait_send()
                arrived = self.slot(z, lax.rem(self.x + self.line - d, self.line))
                seq_copy(arrived, arrived, self.sems[2].at[d, z], self.sems[3].at[d, z],
                         self.z * self.line + lax.rem(self.x + d, self.line)).wait_recv()


def gather_sems(ranks, line):
    long = ranks // line
    return [pltpu.SemaphoreType.DMA((2, long))] * 2 + [pltpu.SemaphoreType.DMA((max(line, 2), long))] * 2


CHUNKS = 4


class TpSum:
    def __init__(self, part, pair, chip, chips, total, send, recv, parts, tp):
        self.refs, self.sems = (part, pair, chip, chips, total), (send, recv)
        self.across, self.core, self.y = parts // 2, lax.rem(tp, 2), tp // 2
        self.sibling = self.y * 2 + (1 - self.core)
        wide = part.shape[1] // 2
        self.rows = part.shape[0] // CHUNKS
        self.mine = pl.ds(pl.multiple_of(self.core * wide, wide), wide)
        self.theirs = pl.ds(pl.multiple_of((1 - self.core) * wide, wide), wide)

    def at(self, n):
        return pl.ds(n * self.rows, self.rows)

    def first(self, n):
        return tp_copy(self.refs[0].at[self.at(n), self.theirs], self.refs[1].at[self.at(n)], self.sems[0].at[0, n],
                       self.sems[1].at[0, n], self.sibling)

    def second(self, d, n):
        return tp_copy(self.refs[2].at[self.at(n)], self.refs[3].at[d, self.at(n)], self.sems[0].at[d, n],
                       self.sems[1].at[d, n], lax.rem(self.y + d, self.across) * 2 + self.core)

    def third(self, n, cols):
        block = self.refs[4].at[self.at(n), cols]
        return tp_copy(block, block, self.sems[0].at[self.across, n], self.sems[1].at[self.across, n], self.sibling)

    def begin(self):
        for n in range(CHUNKS):
            self.first(n).start()

    def middle(self):
        part, pair, chip = self.refs[:3]
        for n in range(CHUNKS):
            at = self.at(n)
            self.first(n).wait_recv()
            chip[at, :] = (part[at, self.mine].astype(F32) + pair[at, :].astype(F32)).astype(BF)
            for d in range(1, self.across):
                self.second(d, n).start()

    def end(self):
        chip, chips, total = self.refs[2:]
        for n in range(CHUNKS):
            at = self.at(n)
            whole = chip[at, :].astype(F32)
            for d in range(1, self.across):
                self.second(d, n).wait_recv()
                whole = whole + chips[d, at, :].astype(F32)
            total[at, self.mine] = whole.astype(BF)
            self.third(n, self.mine).start()
        for n in range(CHUNKS):
            self.third(n, self.theirs).wait_recv()

    def done(self):
        for n in range(CHUNKS):
            self.first(n).wait_send()
            self.third(n, self.mine).wait_send()
            for d in range(1, self.across):
                self.second(d, n).wait_send()


def tp_sum_scratch(tokens, width, parts):
    across = parts // 2
    return [
        pltpu.VMEM((tokens, width // 2), BF),
        pltpu.VMEM((tokens, width // 2), BF),
        pltpu.VMEM((across, tokens, width // 2), BF),
        pltpu.SemaphoreType.DMA((across + 1, CHUNKS)),
        pltpu.SemaphoreType.DMA((across + 1, CHUNKS)),
    ]


def iotas(size):
    return lax.broadcasted_iota(jnp.int32, (size, size), 0), lax.broadcasted_iota(jnp.int32, (size, size), 1)


def decays(decay, beta, size):
    rows, cols = iotas(size)
    log_decay = -0.5 * jnp.exp(-LOG_TWO * decay.astype(F32))
    spread_out = jnp.broadcast_to(log_decay, (size, size))
    total_row = jnp.sum(jnp.where(rows <= cols, spread_out, 0.0), axis=0, keepdims=True)
    total_col = jnp.sum(jnp.where(cols <= rows, spread_out.T, 0.0), axis=1, keepdims=True)
    up_to = rows >= cols
    factors = jnp.where(up_to, jnp.exp(jnp.where(up_to, total_col - total_row, 0.0)), 0.0)
    final = total_col[size - 1 :, :]
    rate = (beta.astype(F32) + 1.0) / 8.0
    return jnp.exp(total_col), jnp.exp(final - total_col), jnp.exp(final), factors, rate


def convolved(ext_ref, taps, b, at, width, tokens):
    return sum(
        taps[j : j + 1, :] * ext_ref[b, pl.ds(HALO - CONV + 1 + j, tokens), pl.ds(at, width)] for j in range(CONV)
    )


def unit_inverses(strict, size):
    rows, cols = iotas(size)

    def below(k):
        return ((rows >> (k + 1)) == (cols >> (k + 1))) & (((rows >> k) & 1) == 1) & (((cols >> k) & 1) == 0)

    eye = (rows == cols).astype(F32)
    found = [eye - jnp.where(below(0), a, 0.0) for a in strict]
    for k in range(1, size.bit_length() - 1):
        moved = [mm3(jnp.where(below(k), a, 0.0), x) for a, x in zip(strict, found)]
        found = [x - mm3(x, m) for x, m in zip(found, moved)]
    return found


def forward_kernel(
    dims, x_in, cot_in, wq, wk, wv, wo, out_in, ffn_in, small_in, decay, beta,
    first, out_t, ffn, x_full, cot_full, small, normed, ext, gate_pre, mixed, gated, attn, start, trans, reach,
    inverse_out, scores_out, written_out, erased_out, query_out, keys_out, factors_out,
    smalls, local, chain_in, chain_out, attn_part, pair, chip, chips,
    small_send, small_recv, tok_send, tok_recv, halo_sems, chain_send, chain_recv, sum_send, sum_recv, *gather,
):
    ranks, parts, line, seqs, tokens, heads = dims
    me, tp = lax.axis_index("seq"), lax.axis_index("tp")
    long = ranks // line
    rows = wq.shape[0]
    q_wide, v_wide = wq.shape[1], wv.shape[1]
    qkv_wide = 2 * q_wide + v_wide
    greet(ranks, parts, me, tp)
    one = Gather(first, rows, ranks, line, me, *gather[0:4])
    two = Gather(out_t, rows, ranks, line, me, *gather[4:8])
    three = Gather(ffn, rows, ranks, line, me, *gather[8:12])

    part_wide = x_in.shape[1]
    own = pl.ds(pl.multiple_of(tp * part_wide, part_wide), part_wide)

    def token_copy(which, src, dst, d):
        return tp_copy(src, dst.at[:, own], tok_send.at[which, d], tok_recv.at[which, d], lax.rem(tp + d, parts))

    def token_wait(which, src, dst, d):
        tp_copy(src, dst.at[:, pl.ds(pl.multiple_of(lax.rem(tp + parts - d, parts) * part_wide, part_wide), part_wide)],
                tok_send.at[which, d], tok_recv.at[which, d], lax.rem(tp + d, parts)).wait_recv()

    def small_copy(d):
        return seq_copy(small_in, smalls.at[d], small_send.at[d], small_recv.at[d], lax.rem(me + d, ranks))

    for d in range(1, parts):
        token_copy(0, x_in, x_full, d).start()
    for d in range(1, ranks):
        small_copy(d).start()
    here = pl.ds(pl.multiple_of(me * rows, rows), rows)
    first[here, 0:q_wide] = wq[...]
    first[here, q_wide : 2 * q_wide] = wk[...]
    first[here, 2 * q_wide : qkv_wide] = wv[...]
    first[here, qkv_wide:] = wo[...]
    one.start()
    out_t[here, :] = out_in[...]
    ffn[here, :] = ffn_in[...]
    for d in range(1, parts):
        token_copy(1, cot_in, cot_full, d).start()
    x_full[:, own] = x_in[...]
    cot_full[:, own] = cot_in[...]

    total = small_in[...].astype(F32)
    for d in range(1, ranks):
        small_copy(d).wait_recv()
        total = total + smalls[d].astype(F32)
    small[...] = total
    for d in range(1, parts):
        token_wait(0, x_in, x_full, d)
    residual = x_full[...].astype(F32)
    scale = lax.rsqrt(jnp.mean(residual * residual, axis=-1, keepdims=True) + EPSILON)
    normed[...] = (residual * scale * small[0:1, 0 : residual.shape[1]]).astype(BF)

    sequence_heads = [(b, h) for b in range(seqs) for h in range(heads)]
    for k in range(1, long):
        one.step(k)
    one.finish()
    two.start()
    tile = 256

    def project(n, carry):
        cols = pl.ds(pl.multiple_of(n * tile, tile), tile)
        found = mm(normed[...], first[:, cols])
        for b in range(seqs):
            ext[b, pl.ds(HALO, tokens), cols] = found[b * tokens : (b + 1) * tokens]
        return carry

    lax.fori_loop(0, qkv_wide // tile, project, 0)

    halo = seq_copy(ext.at[:, pl.ds(tokens, HALO)], ext.at[:, pl.ds(0, HALO)], halo_sems.at[0], halo_sems.at[1],
                    lax.rem(me + 1, ranks))

    @pl.when(me < ranks - 1)
    def _():
        halo.start()

    @pl.when(me == 0)
    def _():
        ext[:, 0:HALO, :] = jnp.zeros((seqs, HALO, qkv_wide), F32)

    def project_gate(n, carry):
        cols = pl.ds(pl.multiple_of(n * tile, tile), tile)
        gate_pre[:, cols] = mm(normed[...], first[:, pl.ds(pl.multiple_of(qkv_wide + n * tile, tile), tile)])
        return carry

    lax.fori_loop(0, v_wide // tile, project_gate, 0)

    @pl.when(me > 0)
    def _():
        halo.wait_recv()

    two.step(1)

    rows_i, cols_i = iotas(tokens)
    state = []
    for b, h in sequence_heads:
        taps = small[2:6, :]
        q_at, k_at, v_at = h * DK, q_wide + h * DK, 2 * q_wide + h * DV
        growth, fade, kept, factors, rate = decays(
            decay[pl.ds(b * tokens, tokens), h : h + 1], beta[pl.ds(b * tokens, tokens), h : h + 1], tokens
        )
        query = convolved(ext, taps[:, q_at : q_at + DK], b, q_at, DK, tokens)
        query = query * sigmoid(query)
        query = query * (lax.rsqrt(jnp.sum(query * query, axis=-1, keepdims=True) + EPSILON) * DK**-0.5)
        keys = convolved(ext, taps[:, k_at : k_at + DK], b, k_at, DK, tokens)
        keys = keys * sigmoid(keys)
        keys = keys * lax.rsqrt(jnp.sum(keys * keys, axis=-1, keepdims=True) + EPSILON)
        values = convolved(ext, taps[:, v_at : v_at + DV], b, v_at, DV, tokens)
        values = values * sigmoid(values)
        strict = jnp.where(rows_i > cols_i, rate * mm3(keys, keys, NT) * factors, 0.0)
        scores = mm3(query, keys, NT) * factors
        query_out[len(state)], keys_out[len(state)] = query, keys
        factors_out[len(state)], scores_out[len(state)] = factors, scores
        state.append((growth, fade, kept, rate, query, keys, values, strict, scores))
    inverses = unit_inverses([s[7] for s in state], tokens)
    for n, (growth, fade, kept, rate, query, keys, values, strict, scores) in enumerate(state):
        inverse = inverses[n]
        written = mm3(inverse, rate * values)
        erased = mm3(inverse, (rate * growth) * keys)
        inverse_out[n], written_out[n], erased_out[n] = inverse, written, erased
        faded = keys * fade
        reach[n] = growth * query - mm3(scores, erased)
        b, h = sequence_heads[n]
        mixed[pl.ds(b * tokens, tokens), h * DV : (h + 1) * DV] = mm3(scores, written)
        trans[n] = jnp.where(rows_i == cols_i, kept, 0.0) - mm3(faded, erased, TN)
        local[n] = mm3(faded, written, TN)

    for k in range(2, long):
        two.step(k)
    two.finish()
    three.start()

    def chain_copy(n):
        return seq_copy(chain_out.at[n], chain_in.at[n], chain_send.at[n], chain_recv.at[n], lax.rem(me + 1, ranks))

    for n in range(len(sequence_heads)):
        @pl.when(me > 0)
        def _():
            chain_copy(n).wait_recv()
            start[n] = chain_in[n]

        @pl.when(me == 0)
        def _():
            start[n] = jnp.zeros((DK, DV), BF)

        @pl.when(me < ranks - 1)
        def _():
            chain_out[n] = (mm2(trans[n], start[n]) + local[n]).astype(BF)
            chain_copy(n).start()

    for n, (b, h) in enumerate(sequence_heads):
        at, cols = pl.ds(b * tokens, tokens), pl.ds(h * DV, DV)
        whole = mixed[at, cols] + mm2(reach[n], start[n])
        mixed[at, cols] = whole
        scale = lax.rsqrt(jnp.mean(whole * whole, axis=-1, keepdims=True) + EPSILON)
        pre = gate_pre[at, cols]
        gated[at, cols] = (whole * scale * small[6:7, cols] * (pre * sigmoid(pre))).astype(BF)

    def give_out(n, carry):
        cols = pl.ds(pl.multiple_of(n * tile, tile), tile)
        attn_part[:, cols] = mm(gated[...], out_t[cols, :], NT).astype(BF)
        return carry

    lax.fori_loop(0, attn_part.shape[1] // tile, give_out, 0)
    heads_sum = TpSum(attn_part, pair, chip, chips, attn, sum_send, sum_recv, parts, tp)
    heads_sum.begin()
    heads_sum.middle()
    heads_sum.end()
    heads_sum.done()

    for k in range(1, long):
        three.step(k)
    three.finish()
    for d in range(1, parts):
        token_wait(1, cot_in, cot_full, d)
        token_copy(0, x_in, x_full, d).wait_send()
        token_copy(1, cot_in, cot_full, d).wait_send()
    for d in range(1, ranks):
        small_copy(d).wait_send()

    @pl.when(me < ranks - 1)
    def _():
        halo.wait_send()
        for n in range(len(sequence_heads)):
            chain_copy(n).wait_send()


def forward_call(dims, x_in, cot_in, wq, wk, wv, wo, out_in, ffn_in, small_in, decay, beta):
    ranks, parts, line, seqs, tokens, heads = dims
    count = seqs * heads
    all_tokens = seqs * tokens
    width = wq.shape[0] * ranks
    rows = wq.shape[0]
    first_wide = wq.shape[1] * 2 + wv.shape[1] * 2
    qkv_wide = wq.shape[1] * 2 + wv.shape[1]
    v_wide = wv.shape[1]
    s = jax.ShapeDtypeStruct
    outs = [
        s((width, first_wide), BF), s((width, out_in.shape[1]), BF), s((width, ffn_in.shape[1]), BF),
        s((all_tokens, width), BF), s((all_tokens, width), BF), s(small_in.shape, F32), s((all_tokens, width), BF),
        s((seqs, HALO + tokens, qkv_wide), F32), s((all_tokens, v_wide), F32), s((all_tokens, v_wide), F32),
        s((all_tokens, v_wide), BF), s((all_tokens, width), BF), s((count, DK, DV), BF), s((count, DK, DK), F32),
        s((count, tokens, DK), F32),
        s((count, tokens, tokens), F32), s((count, tokens, tokens), F32), s((count, tokens, DV), F32),
        s((count, tokens, DK), F32), s((count, tokens, DK), F32), s((count, tokens, DK), F32),
        s((count, tokens, tokens), F32),
    ]
    vmem = pl.BlockSpec(memory_space=pltpu.VMEM)
    dma = pltpu.SemaphoreType.DMA
    scratch = [
        pltpu.VMEM((ranks,) + small_in.shape, BF), pltpu.VMEM((count, DK, DV), F32), pltpu.VMEM((count, DK, DV), BF),
        pltpu.VMEM((count, DK, DV), BF), pltpu.VMEM((all_tokens, width), BF),
    ]
    sums = tp_sum_scratch(all_tokens, width, parts)
    scratch += sums[:3] + [dma((ranks,)), dma((ranks,)), dma((2, parts)), dma((2, parts)), dma((2,)), dma((count,)),
                           dma((count,))] + sums[3:]
    scratch += gather_sems(ranks, line) * 3
    return pl.pallas_call(
        functools.partial(forward_kernel, dims),
        out_shape=outs,
        in_specs=[vmem] * 11,
        out_specs=[vmem] * len(outs),
        scratch_shapes=scratch,
        compiler_params=pltpu.CompilerParams(collective_id=0, has_side_effects=True, vmem_limit_bytes=44 * 2**20),
        name="forward",
    )(x_in, cot_in, wq, wk, wv, wo, out_in, ffn_in, small_in, decay, beta)


class Scatter:
    def __init__(self, grads, rows, ranks, line, me, over, up, down, over_s, over_r, z_s, z_r):
        self.grads, self.rows, self.line, self.long = grads, rows, line, ranks // line
        self.z, self.x = me // line, lax.rem(me, line)
        self.over, self.flows, self.sems = over, (up, down), (over_s, over_r, z_s, z_r)

    def slot(self, z, x):
        return pl.ds(pl.multiple_of((z * self.line + x) * self.rows, self.rows), self.rows)

    def across(self, d, z):
        peer = lax.rem(self.x + d, self.line)
        return seq_copy(self.grads.at[self.slot(z, peer)], self.over.at[d - 1, z], self.sems[0].at[d, z],
                        self.sems[1].at[d, z], self.z * self.line + peer)

    def start(self):
        for n in range(self.long):
            low = lax.rem(self.z + 2 * self.long - 1 - n, self.long)
            high = lax.rem(self.z + 1 + n, self.long)
            target = jnp.where(self.z * 2 >= self.long, high, low)
            for d in range(1, self.line):
                self.across(d, target).start()

    def gathered(self, target):
        value = self.grads[self.slot(target, self.x), :].astype(F32)
        for d in range(1, self.line):
            self.across(d, target).wait_recv()
            value = value + self.over[d - 1, target].astype(F32)
        return value

    def flow(self, way, target):
        block = self.slot(target, self.x)
        there = self.z + (1 if way == 0 else -1)
        there = jnp.clip(there, 0, self.long - 1)
        return seq_copy(self.grads.at[block], self.flows[way].at[target], self.sems[2].at[way, target],
                        self.sems[3].at[way, target], there * self.line + self.x)

    def flow_in(self, way, target):
        landed = self.flows[way].at[target]
        return seq_copy(landed, landed, self.sems[2].at[way, target], self.sems[3].at[way, target],
                        lax.rem(self.z + 1, self.long) * self.line + self.x)

    def step(self, s):
        for way in range(2):
            depth = self.z if way == 0 else self.long - 1 - self.z
            ahead = self.long - 1 - s + depth
            target = ahead if way == 0 else self.long - 1 - ahead

            @pl.when(depth <= s)
            def _():
                block = self.slot(target, self.x)
                self.grads[block, :] = self.gathered(target).astype(BF)

                @pl.when(depth > 0)
                def _():
                    self.flow_in(way, target).wait_recv()
                    self.grads[block, :] = (
                        self.grads[block, :].astype(F32) + self.flows[way][target].astype(F32)
                    ).astype(BF)
                self.flow(way, target).start()

    def finish(self, result):
        result[...] = self.gathered(self.z)

        @pl.when(self.z > 0)
        def _():
            self.flow_in(0, self.z).wait_recv()
            result[...] = result[...] + self.flows[0][self.z].astype(F32)

        @pl.when(self.z < self.long - 1)
        def _():
            self.flow_in(1, self.z).wait_recv()
            result[...] = result[...] + self.flows[1][self.z].astype(F32)
        for s in range(self.long - 1):
            for way in range(2):
                depth = self.z if way == 0 else self.long - 1 - self.z
                ahead = self.long - 1 - s + depth
                target = ahead if way == 0 else self.long - 1 - ahead

                @pl.when(depth <= s)
                def _():
                    self.flow(way, target).wait_send()
        for d in range(1, self.line):
            for z in range(self.long):
                self.across(d, z).wait_send()


def scatter_scratch(ranks, line, rows, width):
    long = ranks // line
    return [
        pltpu.VMEM((max(line - 1, 1), long, rows, width), BF),
        pltpu.VMEM((long, rows, width), BF),
        pltpu.VMEM((long, rows, width), BF),
    ] + [pltpu.SemaphoreType.DMA((max(line, 2), long))] * 2 + [pltpu.SemaphoreType.DMA((2, long))] * 2


def slope_of(values, sig):
    return sig * (1.0 + values * (1.0 - sig))


def low(a, b, dims=NN):
    return mm(a.astype(BF), b.astype(BF), dims)


def backward_kernel(
    dims, x_full, cot_full, first, out_t, ffn, small, normed, ext, gate_pre, mixed, gated, attn, start, trans, reach,
    inverse, scores, written, erased, query, keys, factors, decay, beta,
    block_out, grad_in, late_ffn, late_out, late_mixer, small_out,
    middle, low_two, d_pre, hidden, part_two, sum_two, fed_part, fed_pair, fed_mine, fed_over, turned, d_middle,
    grads_ffn, grads_out, grads_mixer, d_heads, d_gate, chain_in, chain_out, d_conv, halo_in, halo_out, d_proj,
    small_mine, smalls, fed_s, fed_r, chain_s, chain_r, halo_sems, small_s, small_r,
    pair, chip, chips, sum_s, sum_r, pair_one, chip_one, chips_one, sum_s2, sum_r2, *scatters,
):
    ranks, parts, line, seqs, tokens, heads = dims
    me, tp = lax.axis_index("seq"), lax.axis_index("tp")
    long = ranks // line
    model = x_full.shape[1]
    rows = model // ranks
    wide = ffn.shape[1] // 3
    across, core, y = parts // 2, lax.rem(tp, 2), tp // 2
    part_wide = block_out.shape[1]
    q_wide, v_wide = heads * DK, heads * DV
    qkv_wide = 2 * q_wide + v_wide
    tile = 256
    greet(ranks, parts, me, tp)
    ffn_sum = Scatter(grads_ffn, rows, ranks, line, me, *scatters[0:7])
    out_sum = Scatter(grads_out, rows, ranks, line, me, *scatters[7:14])
    mixer_sum = Scatter(grads_mixer, rows, ranks, line, me, *scatters[14:21])

    def tiles(width, step, body):
        def run(n, carry):
            body(pl.ds(pl.multiple_of(n * step, step), step), n)
            return carry
        lax.fori_loop(0, width // step, run, 0)

    middle[...] = x_full[...].astype(F32) + attn[...].astype(F32)
    scale_two = lax.rsqrt(jnp.mean(middle[...] * middle[...], axis=-1, keepdims=True) + EPSILON)
    low_two[...] = (middle[...] * scale_two * small[1:2, 0:model]).astype(BF)

    step = 256 if wide % 256 == 0 else 128

    def feed(cols, n):
        up_cols = pl.ds(pl.multiple_of(wide + n * step, step), step)
        down_cols = pl.ds(pl.multiple_of(2 * wide + n * step, step), step)
        gate = mm(low_two[...], ffn[:, cols])
        up = mm(low_two[...], ffn[:, up_cols])
        d_hidden = mm(cot_full[...], ffn[:, down_cols])
        sig = sigmoid(gate)
        act = gate * sig
        hidden[:, cols] = (act * up).astype(BF)
        d_pre[:, cols] = (d_hidden * up * slope_of(gate, sig)).astype(BF)
        d_pre[:, up_cols] = (d_hidden * act).astype(BF)

    tiles(wide, step, feed)

    def back_two(cols, n):
        part_two[:, cols] = mm(d_pre[...], ffn[cols, 0 : 2 * wide], NT).astype(BF)

    tiles(model, tile, back_two)
    two = TpSum(part_two, pair, chip, chips, sum_two, sum_s, sum_r, parts, tp)
    two.begin()
    turned[...] = low_two[...].T

    def grads_gate_up(cols, n):
        grads_ffn[:, cols] = mm(turned[...], d_pre[:, cols]).astype(BF)

    tiles(2 * wide, step, grads_gate_up)
    two.middle()
    turned[...] = cot_full[...].T

    def grads_down(cols, n):
        grads_ffn[:, pl.ds(pl.multiple_of(2 * wide + n * step, step), step)] = mm(turned[...], hidden[:, cols]).astype(BF)

    tiles(wide, step, grads_down)
    ffn_sum.start()
    two.end()

    def forth(cols, n):
        fed_part[:, cols] = mm(hidden[...], ffn[cols, 2 * wide : 3 * wide], NT).astype(BF)

    tiles(model, tile, forth)

    def fed_first(other):
        cols = pl.ds(pl.multiple_of((other * 2 + 1 - core) * part_wide, part_wide), part_wide)
        return tp_copy(fed_part.at[:, cols], fed_pair.at[other], fed_s.at[0, other], fed_r.at[0, other],
                       y * 2 + 1 - core)

    def fed_second(d):
        peer = lax.rem(y + d, across)
        return tp_copy(fed_mine.at[peer], fed_over.at[d], fed_s.at[1, d], fed_r.at[1, d], peer * 2 + core)

    for other in range(across):
        fed_first(other).start()

    d_two = sum_two[...].astype(F32)
    scale_two = lax.rsqrt(jnp.mean(middle[...] * middle[...], axis=-1, keepdims=True) + EPSILON)
    small_mine[...] = jnp.zeros(small_mine.shape, F32)
    small_mine[1:2, 0:model] = jnp.sum(d_two * middle[...] * scale_two, axis=0, keepdims=True)
    weighted = d_two * small[1:2, 0:model]
    inner = jnp.mean(weighted * middle[...], axis=-1, keepdims=True)
    d_middle[...] = cot_full[...].astype(F32) + scale_two * (weighted - middle[...] * (scale_two * scale_two * inner))
    low_two[...] = d_middle[...].astype(BF)

    for other in range(across):
        fed_first(other).wait_recv()
        cols = pl.ds(pl.multiple_of((other * 2 + core) * part_wide, part_wide), part_wide)
        fed_mine[other] = (fed_part[:, cols].astype(F32) + fed_pair[other].astype(F32)).astype(BF)
    for d in range(1, across):
        fed_second(d).start()

    def back_heads(cols, n):
        d_heads[:, cols] = mm(low_two[...], out_t[:, cols])

    tiles(v_wide, tile, back_heads)

    sequence_heads = [(b, h) for b in range(seqs) for h in range(heads)]
    local = []
    for n, (b, h) in enumerate(sequence_heads):
        at, cols = pl.ds(b * tokens, tokens), pl.ds(h * DV, DV)
        d_gated, pre, whole = d_heads[at, cols], gate_pre[at, cols], mixed[at, cols]
        gain = small[6:7, h * DV : (h + 1) * DV]
        sig = sigmoid(pre)
        scale = lax.rsqrt(jnp.mean(whole * whole, axis=-1, keepdims=True) + EPSILON)
        d_proj[at, pl.ds(qkv_wide + h * DV, DV)] = (d_gated * (whole * scale * gain) * slope_of(pre, sig)).astype(BF)
        d_head = d_gated * (pre * sig)
        small_mine[6:7, cols] += jnp.sum(d_head * whole * scale, axis=0, keepdims=True)
        weighted = d_head * gain
        inner = jnp.mean(weighted * whole, axis=-1, keepdims=True)
        d_mixed = scale * (weighted - whole * (scale * scale * inner))
        d_heads[at, cols] = d_mixed
        local.append(mm3(reach[n], d_mixed, TN))

    def chain_copy(n):
        return seq_copy(chain_out.at[n], chain_in.at[n], chain_s.at[n], chain_r.at[n], lax.rem(me + ranks - 1, ranks))

    for n in range(len(sequence_heads)):
        @pl.when(me < ranks - 1)
        def _():
            chain_copy(n).wait_recv()

        @pl.when(me == ranks - 1)
        def _():
            chain_in[n] = jnp.zeros((DK, DV), BF)

        @pl.when(me > 0)
        def _():
            chain_out[n] = (mm2(trans[n], chain_in[n], TN) + local[n]).astype(BF)
            chain_copy(n).start()

    turned[...] = low_two[...].T

    def grads_output(cols, n):
        grads_out[:, cols] = mm(turned[...], gated[:, cols]).astype(BF)

    tiles(v_wide, tile, grads_output)
    out_sum.start()
    ffn_sum.step(0)

    rows_i, cols_i = iotas(tokens)
    d_conv[...] = jnp.zeros(d_conv.shape, F32)
    for n, (b, h) in enumerate(sequence_heads):
        at, cols = pl.ds(b * tokens, tokens), pl.ds(h * DV, DV)
        growth, fade, kept, unused, rate = decays(
            decay[at, h : h + 1], beta[at, h : h + 1], tokens
        )
        d_out, d_end, state = d_heads[at, cols], chain_in[n], start[n]
        q, k = query[n], keys[n]
        update = written[n] - mm(erased[n].astype(BF), state)
        d_update = low(scores[n], d_out, TN) + mm((k * fade).astype(BF), d_end)
        d_scores = low(d_out, update, NT) * factors[n]
        d_erased = -mm(d_update.astype(BF), state, NT)
        d_written_in = low(inverse[n], d_update, TN)
        d_erased_in = low(inverse[n], d_erased, TN)
        d_strict = -(low(d_written_in, written[n], NT) + low(d_erased_in, erased[n], NT))
        d_dots = jnp.where(rows_i > cols_i, rate * factors[n] * d_strict, 0.0)
        d_query = growth * mm(d_out.astype(BF), state, NT) + low(d_scores, k)
        d_keys = (
            (rate * growth) * d_erased_in + fade * mm(update.astype(BF), d_end, NT)
            + low(d_dots + d_dots.T, k) + low(d_scores, q, TN)
        )
        d_values = rate * d_written_in
        for d_unit, at_col, width, factor in (
            (d_query, h * DK, DK, DK**-0.5), (d_keys, q_wide + h * DK, DK, 1.0), (d_values, 2 * q_wide + h * DV, DV, None),
        ):
            span = pl.ds(at_col, width)
            taps = small[2:6, at_col : at_col + width]
            pre = convolved(ext, taps, b, at_col, width, tokens)
            sig = sigmoid(pre)
            if factor is not None:
                act = pre * sig
                scale = lax.rsqrt(jnp.sum(act * act, axis=-1, keepdims=True) + EPSILON)
                given = d_unit * factor
                d_unit = scale * (given - act * (scale * scale * jnp.sum(act * given, axis=-1, keepdims=True)))
            d_pre_conv = d_unit * slope_of(pre, sig)
            d_conv[b, pl.ds(HALO, tokens), span] = d_pre_conv
            for j in range(CONV):
                small_mine[2 + j : 3 + j, span] += jnp.sum(
                    d_pre_conv * ext[b, pl.ds(HALO - CONV + 1 + j, tokens), span], axis=0, keepdims=True
                )
            halo_out[b, :, span] = sum(
                taps[j : j + 1, :] * d_conv[b, pl.ds(CONV - 1 - j, HALO), span] for j in range(CONV)
            )

    halo = seq_copy(halo_out, halo_in, halo_sems.at[0], halo_sems.at[1], lax.rem(me + ranks - 1, ranks))

    @pl.when(me > 0)
    def _():
        halo.start()

    @pl.when(me == ranks - 1)
    def _():
        halo_in[...] = jnp.zeros(halo_in.shape, F32)

    for s in range(1, long - 1):
        ffn_sum.step(s)
    ffn_sum.finish(late_ffn)

    @pl.when(me < ranks - 1)
    def _():
        halo.wait_recv()

    for b in range(seqs):
        taps = small[2:6, 0:qkv_wide]
        d_ext = sum(taps[j : j + 1, :] * d_conv[b, pl.ds(HALO + CONV - 1 - j, tokens), :] for j in range(CONV))
        edge = jnp.concatenate([jnp.zeros((tokens - HALO, qkv_wide), F32), halo_in[b]], axis=0)
        d_proj[pl.ds(b * tokens, tokens), 0:qkv_wide] = (d_ext + edge).astype(BF)

    def back_one(cols, n):
        part_two[:, cols] = mm(d_proj[...], first[cols, :], NT).astype(BF)

    two.done()
    tiles(model, tile, back_one)
    one = TpSum(part_two, pair_one, chip_one, chips_one, sum_two, sum_s2, sum_r2, parts, tp)
    one.begin()
    turned[...] = normed[...].T

    def grads_first(cols, n):
        grads_mixer[:, cols] = mm(turned[...], d_proj[:, cols]).astype(BF)

    tiles(grads_mixer.shape[1], tile, grads_first)
    mixer_sum.start()
    one.middle()
    for s in range(long - 1):
        out_sum.step(s)
    out_sum.finish(late_out)
    one.end()
    one.done()

    own = pl.ds(pl.multiple_of(tp * part_wide, part_wide), part_wide)
    fed = fed_mine[y].astype(F32)
    for d in range(1, across):
        fed_second(d).wait_recv()
        fed = fed + fed_over[d].astype(F32)
    block_out[...] = (middle[:, own] + fed).astype(BF)

    d_normed = sum_two[...].astype(F32)
    residual = x_full[...].astype(F32)
    scale_one = lax.rsqrt(jnp.mean(residual * residual, axis=-1, keepdims=True) + EPSILON)
    small_mine[0:1, 0:model] = jnp.sum(d_normed * residual * scale_one, axis=0, keepdims=True)
    small_low = smalls.at[0]
    small_low[...] = small_mine[...].astype(BF)

    def small_copy(d):
        return seq_copy(small_low, smalls.at[d], small_s.at[d], small_r.at[d], lax.rem(me + d, ranks))

    for d in range(1, ranks):
        small_copy(d).start()
    weighted = d_normed * small[0:1, 0:model]
    inner = jnp.mean(weighted * residual, axis=-1, keepdims=True)
    middle[...] = d_middle[...] + scale_one * (weighted - residual * (scale_one * scale_one * inner))
    grad_in[...] = middle[:, own]

    for s in range(long - 1):
        mixer_sum.step(s)
    mixer_sum.finish(late_mixer)
    total = smalls[0].astype(F32)
    for d in range(1, ranks):
        small_copy(d).wait_recv()
        total = total + smalls[d].astype(F32)
    small_out[...] = total
    for d in range(1, ranks):
        small_copy(d).wait_send()
    for other in range(across):
        fed_first(other).wait_send()
    for d in range(1, across):
        fed_second(d).wait_send()

    @pl.when(me > 0)
    def _():
        halo.wait_send()
        for n in range(len(sequence_heads)):
            chain_copy(n).wait_send()


def backward_call(dims, inputs, part_wide):
    ranks, parts, line, seqs, tokens, heads = dims
    (x_full, cot_full, first, out_t, ffn, small) = inputs[:6]
    count, all_tokens, model = seqs * heads, seqs * tokens, x_full.shape[1]
    rows, wide = model // ranks, ffn.shape[1] // 3
    qkv_wide = heads * (2 * DK + DV)
    across = parts // 2
    s = jax.ShapeDtypeStruct
    outs = [
        s((all_tokens, part_wide), BF), s((all_tokens, part_wide), F32), s((rows, 3 * wide), F32),
        s((rows, out_t.shape[1]), F32), s((rows, first.shape[1]), F32), s(small.shape, F32),
    ]
    vmem = pl.BlockSpec(memory_space=pltpu.VMEM)
    dma, mem = pltpu.SemaphoreType.DMA, pltpu.VMEM
    sums = tp_sum_scratch(all_tokens, model, parts)
    scratch = [
        mem((all_tokens, model), F32), mem((all_tokens, model), BF), mem((all_tokens, 2 * wide), BF),
        mem((all_tokens, wide), BF), mem((all_tokens, model), BF), mem((all_tokens, model), BF),
        mem((all_tokens, model), BF), mem((across, all_tokens, part_wide), BF), mem((across, all_tokens, part_wide), BF),
        mem((across, all_tokens, part_wide), BF), mem((model, all_tokens), BF), mem((all_tokens, model), F32),
        mem((model, 3 * wide), BF), mem((model, out_t.shape[1]), BF), mem((model, first.shape[1]), BF),
        mem((all_tokens, heads * DV), F32), mem((8, 128), F32), mem((count, DK, DV), BF), mem((count, DK, DV), BF),
        mem((seqs, tokens + 2 * HALO, qkv_wide), F32), mem((seqs, HALO, qkv_wide), F32), mem((seqs, HALO, qkv_wide), F32),
        mem((all_tokens, first.shape[1]), BF), mem(small.shape, F32), mem((ranks,) + small.shape, BF),
        dma((2, max(across, 2))), dma((2, max(across, 2))), dma((count,)), dma((count,)), dma((2,)), dma((ranks,)),
        dma((ranks,)),
    ] + sums + sums
    for width in (3 * wide, out_t.shape[1], first.shape[1]):
        scratch += scatter_scratch(ranks, line, rows, width)
    return pl.pallas_call(
        functools.partial(backward_kernel, dims),
        out_shape=outs,
        in_specs=[vmem] * len(inputs),
        out_specs=[vmem] * len(outs),
        scratch_shapes=scratch,
        compiler_params=pltpu.CompilerParams(collective_id=1, has_side_effects=True, vmem_limit_bytes=60 * 2**20),
        name="backward",
    )(*inputs)


def per_device(
    line,
    block_in,
    out_grad,
    decay_code,
    beta_code,
    norm_gain,
    w_query,
    w_key,
    w_value,
    w_outgate,
    conv_query,
    conv_key,
    conv_value,
    head_gain,
    w_output,
    mlp_gain,
    w_gate,
    w_up,
    w_down,
):
    seqs, tokens, part_wide = block_in.shape
    heads = decay_code.shape[2]
    ranks, parts = lax.axis_size("seq"), lax.axis_size("tp")
    me = lax.axis_index("seq")
    rows = norm_gain.shape[0]
    model = rows * ranks
    hidden = w_gate.shape[1]
    mine = jnp.arange(ranks) == me

    def place(a, lead):
        a = jnp.where(mine[:, None], a.reshape(-1, 1, a.shape[-1]), 0)
        return a.reshape(lead, -1)

    small_wide = max(model, heads * (2 * DK + DV))

    def row(a):
        return jnp.pad(a, ((0, 0), (0, small_wide - a.shape[1])))

    packed = jnp.concatenate(
        [
            row(place(norm_gain, 1)),
            row(place(mlp_gain, 1)),
            row(jnp.concatenate([place(a, CONV) for a in (conv_query, conv_key, conv_value)], axis=1)),
            row(place(head_gain, 1)),
            jnp.zeros((SMALL_ROWS - 3 - CONV, small_wide), BF),
        ],
        axis=0,
    )
    dims = (ranks, parts, line, seqs, tokens, heads)
    padded = -(-hidden // 128) * 128

    def wider(a):
        return jnp.pad(a, ((0, 0), (0, padded - hidden)))

    decay, beta = decay_code.reshape(-1, heads), beta_code.reshape(-1, heads)
    (first, out_t, ffn, x_full, cot_full, small, *rest) = forward_call(
        dims, block_in.reshape(-1, part_wide), out_grad.reshape(-1, part_wide), w_query, w_key, w_value, w_outgate,
        w_output.T, jnp.concatenate([wider(w_gate), wider(w_up), wider(w_down.T)], axis=1), packed, decay, beta,
    )
    block_out, grad_in, late_ffn, late_out, late_mixer, totals = backward_call(
        dims, (x_full, cot_full, first, out_t, ffn, small, *rest, decay, beta), part_wide
    )
    q_wide, v_wide = heads * DK, heads * DV

    def taken(a, width):
        a = a.reshape(-1, ranks, width // ranks)
        return lax.dynamic_index_in_dim(a, me, 1, keepdims=False)

    taps = totals[2 : 2 + CONV]

    def tap_grad(a, width):
        return taken(a.reshape(CONV * heads, width), width).reshape(CONV, heads, -1)

    return (
        block_out.reshape(seqs, tokens, part_wide),
        grad_in.reshape(seqs, tokens, part_wide),
        taken(totals[0, :model], model).reshape(-1),
        late_mixer[:, :q_wide],
        late_mixer[:, q_wide : 2 * q_wide],
        late_mixer[:, 2 * q_wide : 2 * q_wide + v_wide],
        late_mixer[:, 2 * q_wide + v_wide :],
        tap_grad(taps[:, :q_wide], DK),
        tap_grad(taps[:, q_wide : 2 * q_wide], DK),
        tap_grad(taps[:, 2 * q_wide : 2 * q_wide + v_wide], DV),
        taken(totals[2 + CONV, :v_wide].reshape(heads, DV), DV),
        late_out.T,
        taken(totals[1, :model], model).reshape(-1),
        late_ffn[:, :hidden],
        late_ffn[:, padded : padded + hidden],
        late_ffn[:, 2 * padded : 2 * padded + hidden].T,
    )


def solution(mesh):
    spots = [getattr(d, "coords", (0, 0, 0)) for d in mesh.devices[:, 0]]
    line = max(1, len({spot[0] for spot in spots}))
    if mesh.shape["seq"] % line:
        line = 1
    return jax.shard_map(
        functools.partial(per_device, line),
        mesh=mesh,
        in_specs=(
            P(None, "seq", "tp"),
            P(None, "seq", "tp"),
            P(None, "seq", "tp"),
            P(None, "seq", "tp"),
            P("seq"),
            P("seq", "tp"),
            P("seq", "tp"),
            P("seq", "tp"),
            P("seq", "tp"),
            P(None, "tp", "seq"),
            P(None, "tp", "seq"),
            P(None, "tp", "seq"),
            P("tp", "seq"),
            P("tp", "seq"),
            P("seq"),
            P("seq", "tp"),
            P("seq", "tp"),
            P("tp", "seq"),
        ),
        out_specs=(
            P(None, "seq", "tp"),
            P(None, "seq", "tp"),
            P("seq"),
            P("seq", "tp"),
            P("seq", "tp"),
            P("seq", "tp"),
            P("seq", "tp"),
            P(None, "tp", "seq"),
            P(None, "tp", "seq"),
            P(None, "tp", "seq"),
            P("tp", "seq"),
            P("tp", "seq"),
            P("seq"),
            P("seq", "tp"),
            P("seq", "tp"),
            P("tp", "seq"),
        ),
        check_vma=False,
    )
```
